32 devices in a mesh: seq: 8 (over z, x), tp: 4 (over y, core).
Axes of the slice: x: 2, y: 2, z: 4, core: 2. Of those that a mesh axis runs over, the one named last changes fastest.
Arguments:
- hidden_in: bfloat16 [4, 24, 3072], P(None, None, 'seq'), may hold values from -30 to 30
- attn_gain: bfloat16 [3072], P('seq'), may hold values from 0.5 to 1.5
- w_query: bfloat16 [3072, 3072], P('seq', 'tp'), may hold values from -0.109375 to 0.109375
- w_key: bfloat16 [3072, 3072], P('seq', 'tp'), may hold values from -0.109375 to 0.109375
- w_value: bfloat16 [3072, 3072], P('seq', 'tp'), may hold values from -0.109375 to 0.109375
- w_out: bfloat16 [3072, 3072], P('tp', 'seq'), may hold values from -0.109375 to 0.109375
- mlp_gain: bfloat16 [3072], P('seq'), may hold values from 0.5 to 1.5
- w_gate: bfloat16 [3072, 8192], P('seq', 'tp'), may hold values from -0.109375 to 0.109375
- w_up: bfloat16 [3072, 8192], P('seq', 'tp'), may hold values from -0.109375 to 0.109375
- w_down: bfloat16 [8192, 3072], P('tp', 'seq'), may hold values from -0.0625 to 0.0625
- kv_pages: bfloat16 [2, 1664, 32, 3072], P(None, 'seq', None, 'tp'), may hold values from -260 to 260
- lengths: int32 [24], replicated, may hold values from 512 to 2044, as said below
- group_ids: int32 [24], replicated, may hold values from 0 to 1, as said below
- shared_table: int32 [2, 16], replicated, may hold values from 0 to 207, as said below
- own_table: int32 [24, 64], P(None, 'seq'), may hold values from 0 to 207, as said below
Outputs:
- hidden_out: bfloat16 [4, 24, 3072], P(None, None, 'seq')
- new_cache: bfloat16 [2, 4, 24, 3072], P(None, None, None, 'tp')
The draws below stay inside these ranges and needn't reach their ends.
Inputs may be any that keep to these rules, and one draw needn't show every extreme that they name: `lengths`: one request in every draw has the length 2044. `group_ids`: each group number is named by exactly 12 requests. Entries are pages of the pool of the index of seq that holds the page's positions (prompt page p lies on index p // 8); on one index the pages named by shared_table and own_table are all different. `own_table`: entries are pages of the pool of the index of seq that holds the page's positions; entries of logical pages under 16 are never read.
All inputs are finite; a program needn't handle non-finite values.
Results may differ from the reference program's by a relative error of at most 0.0085.
The reference program's roundings to bfloat16 on the way count: a program that leaves them out, or rounds other values in their place, can miss the bound.
Values may be sent and summed in bfloat16 or wider, within the bound.
A program may use at most 192 MiB of HBM per device.

```python
import math
import jax
import jax.numpy as jnp
from jax import lax

D = 3072
HEADS = 32
HEAD_DIM = 96
FF = 8192
GROUPS = 2
GROUP = 12
L_DEV = 256
PAGE = 32
STEPS = 4
SINKS = 4
PROMPT_BLOCKS = 2
REQUESTS = 24
WINDOW = 1024
PPD = 8
PROMPT = 512
PROMPT_PAGES = 16
MAXLEN = 2048
POOL_DEV = 208
POOL = 1664
N_SEQ = 8


def draw_hidden_in(key, part):
    subkeys = jax.random.split(jax.random.fold_in(key, 1), 3)
    array_shape = (STEPS, REQUESTS, D)
    base_draw = jnp.clip(jax.random.normal(subkeys[0], array_shape, jnp.float32), -5.0, 5.0)
    row_scale = jnp.exp(jax.random.uniform(subkeys[1], (STEPS, REQUESTS, 1), jnp.float32, math.log(0.2), math.log(2.0)))
    column_ramp = 1.0 + 2.0 * jnp.arange(D, dtype=jnp.float32) / (D - 1)
    column_rough = jnp.exp(jax.random.uniform(subkeys[2], (D,), jnp.float32, math.log(0.5), math.log(2.0)))
    return (0.5 * base_draw * row_scale * column_ramp * column_rough).astype(jnp.bfloat16)


def draw_kv_pages(key, part):
    subkeys = jax.random.split(jax.random.fold_in(key, 2), 1)
    array_shape = (2, POOL, PAGE, HEADS * HEAD_DIM)
    level = jnp.array([1.0, 2.0], jnp.float32)[:, None, None, None]
    base_draw = jnp.clip(jax.random.normal(subkeys[0], array_shape, jnp.float32), -6.0, 6.0) * level
    return base_draw.astype(jnp.bfloat16)


def draw_lengths(key, part):
    first_key, second_key = jax.random.split(jax.random.fold_in(key, 5))
    drawn = jax.random.randint(first_key, (REQUESTS,), PROMPT, MAXLEN - STEPS + 1)
    longest = jax.random.randint(second_key, (), 0, REQUESTS)
    return jnp.where(jnp.arange(REQUESTS) == longest, MAXLEN - STEPS, drawn).astype(jnp.int32)


def draw_group_ids(key, part):
    shuffled = jax.random.permutation(jax.random.fold_in(key, 3), REQUESTS)
    return (shuffled // GROUP).astype(jnp.int32)


def page_layout(key):
    seed_list = jax.random.split(jax.random.fold_in(key, 11), N_SEQ)
    shuffled = jax.vmap(lambda single: jax.random.permutation(single, POOL_DEV))(seed_list).astype(jnp.int32)
    own_pages = shuffled[:, GROUPS * PPD:].reshape(N_SEQ, REQUESTS, PPD)
    own_pages = jnp.transpose(own_pages, (1, 0, 2)).reshape(REQUESTS, N_SEQ * PPD)
    shared_pages = shuffled[:PROMPT_BLOCKS, :GROUPS * PPD].reshape(PROMPT_BLOCKS, GROUPS, PPD)
    shared_pages = jnp.transpose(shared_pages, (1, 0, 2)).reshape(GROUPS, PROMPT_BLOCKS * PPD)
    return (shared_pages, own_pages)


def draw_shared_table(key, part):
    return page_layout(key)[0]


def draw_own_table(key, part):
    return page_layout(key)[1]


def shard_levels(key, extent, shards, least, largest):
    level = 1.0
    for dim, shards_of in shards:
        draws = jax.random.uniform(jax.random.fold_in(jax.random.fold_in(key, 6), dim), (shards_of,), jnp.float32, least / len(shards), largest / len(shards))
        level = level * jnp.repeat(jnp.exp(draws), extent[dim] // shards_of).reshape((-1,) + (1,) * (len(extent) - 1 - dim))
    return level


def bell_draw(own_key, dims, deviation, reach, cuts=(), kind=jnp.bfloat16):
    result = jax.random.normal(own_key, dims, jnp.float32) * deviation
    if len(cuts) > 0:
        result = shard_levels(own_key, dims, cuts, -0.22, 0.18) * result
    return jnp.clip(result, min=-reach, max=reach).astype(kind)


def setup_inputs(seed: int = 0) -> dict:
    splits = jax.random.split(jax.random.key(seed), 16)
    hidden_in = draw_hidden_in(jax.random.fold_in(splits[15], 71), 0)
    attn_gain = jnp.clip(1.0 + 0.1 * jax.random.normal(splits[1], (D,), jnp.float32), 0.5, 1.5).astype(jnp.bfloat16)
    w_query = bell_draw(splits[2], (D, HEADS * HEAD_DIM), D ** -0.5, 0.109375, ((0, 8), (1, 4)))
    w_key = bell_draw(splits[3], (D, HEADS * HEAD_DIM), D ** -0.5, 0.109375, ((0, 8), (1, 4)))
    w_value = bell_draw(splits[4], (D, HEADS * HEAD_DIM), D ** -0.5, 0.109375, ((0, 8), (1, 4)))
    w_out = bell_draw(splits[5], (HEADS * HEAD_DIM, D), (HEADS * HEAD_DIM) ** -0.5, 0.109375, ((0, 4), (1, 8)))
    mlp_gain = jnp.clip(1.0 + 0.1 * jax.random.normal(splits[6], (D,), jnp.float32), 0.5, 1.5).astype(jnp.bfloat16)
    w_gate = bell_draw(splits[7], (D, FF), D ** -0.5, 0.109375, ((0, 8), (1, 4)))
    w_up = bell_draw(splits[8], (D, FF), D ** -0.5, 0.109375, ((0, 8), (1, 4)))
    w_down = bell_draw(splits[9], (FF, D), FF ** -0.5, 0.0625, ((0, 4), (1, 8)))
    kv_pages = draw_kv_pages(jax.random.fold_in(splits[15], 71), 0)
    lengths = draw_lengths(jax.random.fold_in(splits[15], 71), 0)
    group_ids = draw_group_ids(jax.random.fold_in(splits[15], 71), 0)
    shared_table = draw_shared_table(jax.random.fold_in(splits[15], 71), 0)
    own_table = draw_own_table(jax.random.fold_in(splits[15], 71), 0)
    return dict(hidden_in=hidden_in, attn_gain=attn_gain, w_query=w_query, w_key=w_key, w_value=w_value, w_out=w_out, mlp_gain=mlp_gain, w_gate=w_gate, w_up=w_up, w_down=w_down, kv_pages=kv_pages, lengths=lengths, group_ids=group_ids, shared_table=shared_table, own_table=own_table)


EPSILON = 1e-05
ROPE_BASE = 10000.0
NEGATIVE = -1e+30

def rotate(vector, position):
    halfway = vector.shape[-1] // 2
    frequency = ROPE_BASE ** (-(jnp.arange(halfway, dtype=jnp.float32) * 2.0 / vector.shape[-1]))
    angles = position[..., None].astype(jnp.float32) * frequency
    cosine = jnp.cos(angles)
    sine_part = jnp.sin(angles)
    first_half = vector[..., :halfway]
    second_half = vector[..., halfway:]
    return jnp.concatenate([first_half * cosine - second_half * sine_part, second_half * cosine + first_half * sine_part], -1)

def reference(hidden_in, attn_gain, w_query, w_key, w_value, w_out, mlp_gain, w_gate, w_up, w_down, kv_pages, lengths, group_ids, shared_table, own_table):
    score_scale = 1.0 / math.sqrt(HEAD_DIM)
    residual = hidden_in.astype(jnp.float32).reshape(STEPS * REQUESTS, D)
    inv_rms = lax.rsqrt(lax.optimization_barrier(jnp.sum(residual * residual, axis=-1)) / D + EPSILON)
    normed = (residual * attn_gain.astype(jnp.float32)).astype(jnp.bfloat16)

    def project(weight):
        product = jnp.dot(normed, weight, preferred_element_type=jnp.float32) * inv_rms[:, None]
        return product.reshape(STEPS, REQUESTS, HEADS, HEAD_DIM)
    step_col = jnp.arange(STEPS, dtype=jnp.int32)
    where_now = lengths[None, :] + step_col[:, None]
    queries = rotate(project(w_query), where_now[:, :, None]).astype(jnp.bfloat16)
    key_new = rotate(project(w_key), where_now[:, :, None]).astype(jnp.bfloat16)
    value_new = project(w_value).astype(jnp.bfloat16)
    new_cache = jnp.stack([key_new.reshape(STEPS, REQUESTS, HEADS * HEAD_DIM), value_new.reshape(STEPS, REQUESTS, HEADS * HEAD_DIM)])
    offsets = jnp.arange(WINDOW - 1, dtype=jnp.int32)
    sink_place = jnp.arange(SINKS, dtype=jnp.int32)
    new_live = step_col[None, :] <= step_col[:, None]
    is_sink = jnp.arange(SINKS + WINDOW - 1, dtype=jnp.int32) < SINKS

    def attend(request_items):
        length, group_id, own_row, query_rows, key_rows, value_rows = request_items
        placed = jnp.concatenate([sink_place, length - WINDOW + 1 + offsets])
        clamped = jnp.maximum(placed, 0)
        logical = clamped // PAGE
        shared_row = shared_table[group_id]
        page_id = jnp.where(logical < PROMPT_PAGES, shared_row[jnp.minimum(logical, PROMPT_PAGES - 1)], own_row[logical])
        pool_page = clamped // L_DEV * POOL_DEV + page_id
        offset_in = clamped % PAGE
        cached_keys = kv_pages[0, pool_page, offset_in].reshape(-1, HEADS, HEAD_DIM)
        cached_values = kv_pages[1, pool_page, offset_in].reshape(-1, HEADS, HEAD_DIM)
        all_keys = jnp.concatenate([cached_keys, key_rows], 0).astype(jnp.float32)
        all_values = jnp.concatenate([cached_values, value_rows], 0).astype(jnp.float32)
        cached_live = is_sink[None, :] | (placed[None, :] >= SINKS) & (placed[None, :] > length + step_col[:, None] - WINDOW)
        is_live = jnp.concatenate([cached_live, new_live], 1)
        scores = jnp.einsum('shd,khd->shk', query_rows.astype(jnp.float32), all_keys) * score_scale
        scores = jnp.where(is_live[:, None, :], scores, NEGATIVE)
        score_peak = lax.optimization_barrier(jnp.max(scores, axis=-1))
        weights = jnp.where(is_live[:, None, :], jnp.exp(scores - score_peak[..., None]), 0.0)
        weight_sum = lax.optimization_barrier(jnp.sum(weights, axis=-1))
        summed = jnp.einsum('shk,khd->shd', weights, all_values)
        return summed / weight_sum[..., None]
    attended = lax.map(attend, (lengths, group_ids, own_table, jnp.swapaxes(queries, 0, 1), jnp.swapaxes(key_new, 0, 1), jnp.swapaxes(value_new, 0, 1)))
    attn = jnp.swapaxes(attended, 0, 1).astype(jnp.bfloat16).reshape(STEPS * REQUESTS, HEADS * HEAD_DIM)
    mid_rows = residual + jnp.dot(attn, w_out, preferred_element_type=jnp.float32)
    mlp_in = (mid_rows * mlp_gain.astype(jnp.float32)).astype(jnp.bfloat16)
    inv_mid = lax.rsqrt(lax.optimization_barrier(jnp.sum(mid_rows * mid_rows, axis=-1)) / D + EPSILON)[:, None]
    gate = jnp.dot(mlp_in, w_gate, preferred_element_type=jnp.float32) * inv_mid
    upward = jnp.dot(mlp_in, w_up, preferred_element_type=jnp.float32) * inv_mid
    activated = (jax.nn.silu(gate) * upward).astype(jnp.bfloat16)
    hidden_out = (mid_rows + jnp.dot(activated, w_down, preferred_element_type=jnp.float32)).astype(jnp.bfloat16)
    return (hidden_out.reshape(STEPS, REQUESTS, D), new_cache)
```

```python
import functools
import math

import jax
import jax.numpy as jnp
from jax import lax
from jax.experimental import pallas as pl
from jax.experimental.pallas import tpu as pltpu
from jax.sharding import PartitionSpec as P

D = 3072
HEAD_DIM = 96
SINKS = 4
WINDOW = 1024


EPSILON = 1e-05
ROPE_BASE = 10000.0
NEGATIVE = -1e30


def rotate(vector, position):
    halfway = vector.shape[-1] // 2
    frequency = ROPE_BASE ** (-(jnp.arange(halfway, dtype=jnp.float32) * 2.0 / vector.shape[-1]))
    angles = position[..., None].astype(jnp.float32) * frequency
    cosine = jnp.cos(angles)
    sine_part = jnp.sin(angles)
    first_half = vector[..., :halfway]
    second_half = vector[..., halfway:]
    return jnp.concatenate(
        [
            first_half * cosine - second_half * sine_part,
            second_half * cosine + first_half * sine_part,
        ],
        -1,
    )


def seq_total(partial_value, squares):
    return lax.psum((partial_value, squares), "seq")


def head_total(partial_value):
    return lax.psum(partial_value, "tp")


def body(
    hidden_in,
    attn_gain,
    w_query,
    w_key,
    w_value,
    w_out,
    mlp_gain,
    w_gate,
    w_up,
    w_down,
    kv_pages,
    lengths,
    group_ids,
    shared_table,
    own_table,
):
    seq_index = lax.axis_index("seq")
    step_count = hidden_in.shape[0]
    requests = hidden_in.shape[1]
    local_width = hidden_in.shape[2]
    head_cols = w_query.shape[1]
    local_heads = head_cols // HEAD_DIM
    unit_cols = w_gate.shape[1]
    page_rows = kv_pages.shape[2]
    local_pages = own_table.shape[1]
    block_len = local_pages * page_rows
    group_count = shared_table.shape[0]
    prompt_pages = shared_table.shape[1]
    score_scale = 1.0 / math.sqrt(HEAD_DIM)
    flat_rows = step_count * requests
    logical = seq_index * local_pages + jnp.arange(local_pages, dtype=jnp.int32)
    group_pick = (group_ids[:, None] == jnp.arange(group_count, dtype=jnp.int32)[None, :]).astype(
        jnp.int32
    )
    group_rows = jnp.sum(group_pick[:, :, None] * shared_table[None, :, :], axis=1)
    column_pick = (logical[:, None] == jnp.arange(prompt_pages, dtype=jnp.int32)[None, :]).astype(
        jnp.int32
    )
    shared_local = jnp.sum(group_rows[:, None, :] * column_pick[None, :, :], axis=2)
    physical = jnp.where(logical[None, :] < prompt_pages, shared_local, own_table)
    gathered = kv_pages[:, physical]
    cached_keys = gathered[0].reshape(requests, block_len, local_heads, HEAD_DIM)
    cached_values = (
        gathered[1].reshape(requests, block_len, local_heads, HEAD_DIM).astype(jnp.float32)
    )
    positions = seq_index * block_len + jnp.arange(block_len, dtype=jnp.int32)
    step_ids = jnp.arange(step_count, dtype=jnp.int32)
    owner_new = jnp.transpose((lengths[None, :] + step_ids[:, None]) // block_len == seq_index)
    attn_scale = attn_gain.astype(jnp.float32)
    mlp_scale = mlp_gain.astype(jnp.float32)
    w_pair = jnp.concatenate([w_gate, w_up], axis=1)
    residual = hidden_in.astype(jnp.float32).reshape(flat_rows, local_width)
    normed = (residual * attn_scale).astype(jnp.bfloat16)
    squares = jnp.sum(residual * residual, axis=-1)
    where_now = lengths[None, :] + step_ids[:, None]
    w_qkv = jnp.concatenate([w_query, w_key, w_value], axis=1)
    partial_value = jnp.dot(normed, w_qkv, preferred_element_type=jnp.float32)
    summed, square_sum = seq_total(partial_value, squares)
    inv_rms = lax.rsqrt(square_sum / D + EPSILON)
    projected = (summed * inv_rms[:, None]).reshape(step_count, requests, 3, local_heads, HEAD_DIM)
    queries = rotate(projected[:, :, 0], where_now[:, :, None]).astype(jnp.bfloat16)
    key_new = (
        rotate(projected[:, :, 1], where_now[:, :, None])
        .astype(jnp.bfloat16)
        .reshape(step_count, requests, head_cols)
    )
    value_new = projected[:, :, 2].astype(jnp.bfloat16).reshape(step_count, requests, head_cols)
    store_keys = key_new.reshape(step_count, requests, local_heads, HEAD_DIM)
    store_values = value_new.reshape(step_count, requests, local_heads, HEAD_DIM).astype(
        jnp.float32
    )
    in_window = positions[None, None, :] > lengths[None, :, None] + step_ids[:, None, None] - WINDOW
    is_live = (positions[None, None, :] < lengths[None, :, None]) & (
        (positions[None, None, :] < SINKS) | in_window
    )
    new_live = (step_ids[None, None, :] <= step_ids[:, None, None]) & owner_new[None, :, :]
    scores = (
        jnp.einsum("tbhd,bkhd->tbhk", queries, cached_keys, preferred_element_type=jnp.float32)
        * score_scale
    )
    new_scores = (
        jnp.einsum("tbhd,sbhd->tbhs", queries, store_keys, preferred_element_type=jnp.float32)
        * score_scale
    )
    scores = jnp.where(is_live[:, :, None, :], scores, NEGATIVE)
    new_scores = jnp.where(new_live[:, :, None, :], new_scores, NEGATIVE)
    local_peak = jnp.maximum(jnp.max(scores, axis=-1), jnp.max(new_scores, axis=-1))
    score_peak = lax.pmax(local_peak, "seq")
    weights = jnp.where(is_live[:, :, None, :], jnp.exp(scores - score_peak[..., None]), 0.0)
    new_weights = jnp.where(
        new_live[:, :, None, :], jnp.exp(new_scores - score_peak[..., None]), 0.0
    )
    weight_sum = jnp.sum(weights, axis=-1) + jnp.sum(new_weights, axis=-1)
    weighted = jnp.einsum("tbhk,bkhd->tbhd", weights, cached_values) + jnp.einsum(
        "tbhs,sbhd->tbhd", new_weights, store_values
    )
    local_sum = weight_sum
    local_weighted = weighted
    weight_sum, weighted = lax.psum((local_sum, local_weighted), "seq")
    attn = (weighted / weight_sum[..., None]).astype(jnp.bfloat16).reshape(flat_rows, head_cols)
    mid_rows = residual + head_total(jnp.dot(attn, w_out, preferred_element_type=jnp.float32))
    mlp_in = (mid_rows * mlp_scale).astype(jnp.bfloat16)
    mid_squares = jnp.sum(mid_rows * mid_rows, axis=-1)
    gate_up = jnp.dot(mlp_in, w_pair, preferred_element_type=jnp.float32)
    pair_sum, mid_sum = seq_total(gate_up, mid_squares)
    inv_mid = lax.rsqrt(mid_sum / D + EPSILON)[:, None]
    activated = (
        jax.nn.silu(pair_sum[:, :unit_cols] * inv_mid) * (pair_sum[:, unit_cols:] * inv_mid)
    ).astype(jnp.bfloat16)
    result = (
        mid_rows + head_total(jnp.dot(activated, w_down, preferred_element_type=jnp.float32))
    ).astype(jnp.bfloat16)
    hidden_out = result.reshape(step_count, requests, local_width)
    return (hidden_out, jnp.stack([key_new, value_new]))


MESH_ID = pl.DeviceIdType.MESH
LANES = 128
HALF_LANES = 64


def greet(axes):
    barrier = pltpu.get_barrier_semaphore()
    total = 0
    for axis, size in axes:
        me = lax.axis_index(axis)
        for step in range(1, size):
            pl.semaphore_signal(
                barrier,
                inc=1,
                device_id={axis: lax.rem(me + step, size)},
                device_id_type=MESH_ID,
            )
            total += 1
    pl.semaphore_wait(barrier, total)


def send(source, target, axis, peer, send_sem, recv_sem):
    copy = pltpu.make_async_remote_copy(
        src_ref=source,
        dst_ref=target,
        send_sem=send_sem,
        recv_sem=recv_sem,
        device_id={axis: peer},
        device_id_type=MESH_ID,
    )
    copy.start()
    return copy


def project_kernel(
    n,
    x_ref,
    gain_ref,
    wq_ref,
    wk_ref,
    wv_ref,
    cos_ref,
    sin_ref,
    out_ref,
    partial,
    chunks,
    landed,
    shared,
    send_a,
    recv_a,
    send_b,
    recv_b,
):
    me = lax.axis_index("seq")
    rows = chunks.shape[1]
    cols = wq_ref.shape[1]
    width = 3 * cols
    steps = out_ref.shape[1]
    x = x_ref[...].astype(jnp.float32)
    normed = (x * gain_ref[...].astype(jnp.float32)).astype(jnp.bfloat16)
    squares = jnp.sum(x * x, axis=-1, keepdims=True)
    for index, weight in enumerate((wq_ref, wk_ref, wv_ref)):
        partial[:, index * cols : (index + 1) * cols] = jnp.dot(
            normed, weight[...], preferred_element_type=jnp.float32
        )
    partial[:, width:] = jnp.broadcast_to(squares, (x.shape[0], LANES))
    for j in range(n):
        chunks[j] = partial[j * rows : (j + 1) * rows, :]
    greet((("seq", n),))
    copies = []
    for d in range(1, n):
        peer = lax.rem(me + d, n)
        copies.append(
            send(chunks.at[peer], landed.at[d - 1], "seq", peer, send_a.at[d - 1], recv_a.at[d - 1])
        )
    total = chunks[me]
    for d in range(1, n):
        copies[d - 1].wait_recv()
        total = total + landed[d - 1]
    inv_rms = lax.rsqrt(total[:, width : width + 1] / D + EPSILON)
    projected = total[:, :width] * inv_rms
    lane = lax.broadcasted_iota(jnp.int32, (rows, cols), 1)
    early = lax.rem(lane, HEAD_DIM) < HEAD_DIM // 2
    cosine = cos_ref[me]
    sine = sin_ref[me]

    def turn(vector):
        ahead = pltpu.roll(vector, cols - HEAD_DIM // 2, 1)
        behind = pltpu.roll(vector, HEAD_DIM // 2, 1)
        return vector * cosine + jnp.where(early, -ahead, behind) * sine

    ready = jnp.concatenate(
        [
            turn(projected[:, :cols]),
            turn(projected[:, cols : 2 * cols]),
            projected[:, 2 * cols :],
        ],
        axis=1,
    ).astype(jnp.bfloat16)
    shared[me, 0:rows] = ready
    outgoing = []
    for d in range(1, n):
        peer = lax.rem(me + d, n)
        outgoing.append(
            send(shared.at[me], shared.at[me], "seq", peer, send_b.at[d - 1], recv_b.at[d - 1])
        )
    for copy in copies:
        copy.wait_send()
    for copy in outgoing:
        copy.wait_recv()
    for j in range(n):
        held = shared[j].astype(jnp.float32)
        for i in range(rows // steps):
            out_ref[j * (rows // steps) + i] = held[i * steps : (i + 1) * steps]
    for copy in outgoing:
        copy.wait_send()


def attend_kernel(
    lengths_ref, pages_ref, qkv_ref, kv_ref, out_ref, pages, page_sem
):
    seq_index = lax.axis_index("seq")
    requests, steps = qkv_ref.shape[0], qkv_ref.shape[1]
    cols = pages.shape[-1]
    block_len = pages.shape[2]
    local_pages = page_sem.shape[1]
    page_rows = block_len // local_pages
    heads = cols // HEAD_DIM
    base = seq_index * block_len
    scale = 1.0 / math.sqrt(HEAD_DIM)

    def page_copy(b, p):
        return pltpu.make_async_copy(
            kv_ref.at[:, pages_ref[b, p]],
            pages.at[b, :, pl.ds(p * page_rows, page_rows)],
            page_sem.at[b, p],
        )

    def is_used(b):
        length = lengths_ref[b]
        return (base < length + steps) & ((base < SINKS) | (base + block_len > length - WINDOW))

    @pl.loop(0, requests)
    def _(b):
        @pl.when(is_used(b))
        def _():
            for p in range(local_pages):
                page_copy(b, p).start()

    head_row = lax.broadcasted_iota(jnp.int32, (heads, cols), 0) * HEAD_DIM
    head_lane = lax.broadcasted_iota(jnp.int32, (heads, cols), 1)
    own = jnp.where((head_lane >= head_row) & (head_lane < head_row + HEAD_DIM), 1.0, 0.0)
    stat_lane = lax.broadcasted_iota(jnp.int32, (heads, LANES), 1)
    stat_row = lax.broadcasted_iota(jnp.int32, (heads, LANES), 0)
    pick_peak = jnp.where(stat_lane == stat_row, 1.0, 0.0)
    pick_sum = jnp.where(stat_lane == stat_row + HALF_LANES, 1.0, 0.0)
    row_step = lax.broadcasted_iota(jnp.int32, (steps * heads, block_len), 0) // heads
    place = base + lax.broadcasted_iota(jnp.int32, (steps * heads, block_len), 1)
    page_row = lax.broadcasted_iota(jnp.int32, (page_rows, cols), 0)
    idle_lane = lax.broadcasted_iota(jnp.int32, (steps, cols + LANES), 1)
    idle = jnp.where((idle_lane >= cols) & (idle_lane < cols + HALF_LANES), NEGATIVE, 0.0)

    @pl.loop(0, requests)
    def _(b):
        used = is_used(b)

        @pl.when(jnp.logical_not(used))
        def _():
            out_ref[b] = idle

        @pl.when(used)
        def _():
            length = lengths_ref[b]
            for p in range(local_pages):
                page_copy(b, p).wait()
            for u in range(steps):
                spot = length + u - base

                @pl.when((spot >= 0) & (spot < block_len))
                def _():
                    top = pl.multiple_of(spot // page_rows * page_rows, page_rows)
                    hit = page_row == spot - top
                    for kind in range(2):
                        fresh = qkv_ref[b, u : u + 1, (kind + 1) * cols : (kind + 2) * cols]
                        old = pages[b, kind, pl.ds(top, page_rows), :].astype(jnp.float32)
                        pages[b, kind, pl.ds(top, page_rows), :] = jnp.where(
                            hit, fresh, old
                        ).astype(jnp.bfloat16)

            wide = jnp.concatenate(
                [qkv_ref[b, t : t + 1, :cols] * own for t in range(steps)], axis=0
            ).astype(jnp.bfloat16)
            scores = (
                lax.dot_general(
                    wide,
                    pages[b, 0],
                    (((1,), (1,)), ((), ())),
                    preferred_element_type=jnp.float32,
                )
                * scale
            )
            reach = length + row_step
            live = (place <= reach) & ((place < SINKS) | (place > reach - WINDOW))
            scores = jnp.where(live, scores, NEGATIVE)
            peak = jnp.max(scores, axis=-1, keepdims=True)
            weights = jnp.where(live, jnp.exp(scores - peak), 0.0)
            weight_sum = jnp.sum(weights, axis=-1, keepdims=True)
            coarse = weights.astype(jnp.bfloat16)
            fine = (weights - coarse.astype(jnp.float32)).astype(jnp.bfloat16)
            both = jnp.dot(
                jnp.concatenate([coarse, fine], axis=0),
                pages[b, 1],
                preferred_element_type=jnp.float32,
            )
            weighted = both[: steps * heads] + both[steps * heads :]
            for t in range(steps):
                part = slice(t * heads, (t + 1) * heads)
                out_ref[b, t : t + 1, :cols] = jnp.sum(weighted[part] * own, axis=0, keepdims=True)
                out_ref[b, t : t + 1, cols:] = jnp.sum(
                    peak[part] * pick_peak + weight_sum[part] * pick_sum, axis=0, keepdims=True
                )


def finish_kernel(
    n,
    m,
    att_ref,
    x_ref,
    gain_ref,
    wo_ref,
    wg_ref,
    wu_ref,
    wd_ref,
    out_ref,
    chunks,
    landed,
    shared,
    flat,
    mid_landed,
    mid_all,
    pair_out,
    pair_landed,
    square_out,
    square_landed,
    acts,
    down_landed,
    last,
    send_a,
    recv_a,
    send_b,
    recv_b,
    send_c,
    recv_c,
    send_d,
    recv_d,
    send_e,
    recv_e,
    send_s,
    recv_s,
    send_f,
    recv_f,
    send_g,
    recv_g,
    send_h,
    recv_h,
):
    me = lax.axis_index("seq")
    rank = lax.axis_index("tp")
    rows = chunks.shape[1]
    steps = att_ref.shape[1]
    cols = wo_ref.shape[0]
    group = mid_all.shape[1]
    flat_rows = flat.shape[0]
    local_width = flat.shape[1]
    units = acts.shape[2]
    per = rows // steps
    for j in range(n):
        for i in range(per):
            chunks[j, i * steps : (i + 1) * steps] = att_ref[j * per + i]
    greet((("seq", n), ("tp", m)))
    copies = []
    for d in range(1, n):
        peer = lax.rem(me + d, n)
        copies.append(
            send(chunks.at[peer], landed.at[d - 1], "seq", peer, send_a.at[d - 1], recv_a.at[d - 1])
        )
    for copy in copies:
        copy.wait_recv()
    arrived = [chunks[me]] + [landed[d - 1] for d in range(1, n)]
    stats = [value[:, cols:] for value in arrived]
    lane = lax.broadcasted_iota(jnp.int32, (rows, LANES), 1)
    is_peak = lane < HALF_LANES
    peaks = [jnp.where(is_peak, value, 0.0) for value in stats]
    top = functools.reduce(jnp.maximum, peaks)
    factors = [jnp.exp(value - top) for value in peaks]
    sums = [pltpu.roll(value, HALF_LANES, 1) for value in stats]
    total_sum = functools.reduce(lambda a, b: a + b, [f * s for f, s in zip(factors, sums)])
    heads = cols // HEAD_DIM
    inverse = 1.0 / jnp.where(lane < heads, total_sum, 1.0)
    spread_row = lax.broadcasted_iota(jnp.int32, (LANES, cols), 0) * HEAD_DIM
    spread_lane = lax.broadcasted_iota(jnp.int32, (LANES, cols), 1)
    spread = jnp.where(
        (spread_lane >= spread_row) & (spread_lane < spread_row + HEAD_DIM), 1.0, 0.0
    )
    attn = jnp.zeros((rows, cols), jnp.float32)
    for factor, value in zip(factors, arrived):
        share = jnp.where(lane < heads, factor * inverse, 0.0)
        attn = attn + value[:, :cols] * jnp.dot(
            share, spread, precision=lax.Precision.HIGHEST, preferred_element_type=jnp.float32
        )
    shared[me, 0:rows] = attn.astype(jnp.bfloat16)
    outgoing = []
    for d in range(1, n):
        peer = lax.rem(me + d, n)
        outgoing.append(
            send(shared.at[me], shared.at[me], "seq", peer, send_b.at[d - 1], recv_b.at[d - 1])
        )
    for copy in copies:
        copy.wait_send()
    for copy in outgoing:
        copy.wait_recv()
    padded = shared.shape[1]
    product = jnp.dot(
        shared[...].reshape(n * padded, cols), wo_ref[...], preferred_element_type=jnp.float32
    )
    for j in range(n):
        flat[j * rows : (j + 1) * rows, :] = product[j * padded : j * padded + rows]
    for copy in outgoing:
        copy.wait_send()

    def tp_scatter(target, send_sem, recv_sem):
        started = []
        for d in range(1, m):
            peer = lax.rem(rank + d, m)
            first = pl.multiple_of(peer * group, group)
            started.append(
                send(
                    flat.at[pl.ds(first, group)],
                    target.at[d - 1],
                    "tp",
                    peer,
                    send_sem.at[d - 1],
                    recv_sem.at[d - 1],
                )
            )
        total = flat[pl.ds(pl.multiple_of(rank * group, group), group), :]
        for d in range(1, m):
            started[d - 1].wait_recv()
            total = total + target[d - 1]
        for copy in started:
            copy.wait_send()
        return total

    def tp_gather(buffer, send_sem, recv_sem):
        started = []
        for d in range(1, m):
            peer = lax.rem(rank + d, m)
            started.append(
                send(
                    buffer.at[rank],
                    buffer.at[rank],
                    "tp",
                    peer,
                    send_sem.at[d - 1],
                    recv_sem.at[d - 1],
                )
            )
        for copy in started:
            copy.wait()

    own_rows = pl.ds(pl.multiple_of(rank * group, group), group)
    mid_own = x_ref[own_rows, :] + tp_scatter(mid_landed, send_c, recv_c)
    mid_all[rank] = mid_own
    tp_gather(mid_all, send_d, recv_d)
    mid = mid_all[...].reshape(flat_rows, local_width)
    mlp_in = (mid * gain_ref[...].astype(jnp.float32)).astype(jnp.bfloat16)
    square_out[...] = lax.dot_general(
        jnp.ones((8, local_width), jnp.float32),
        mid * mid,
        (((1,), (1,)), ((), ())),
        precision=lax.Precision.HIGHEST,
        preferred_element_type=jnp.float32,
    )
    squares = []
    for d in range(1, n):
        peer = lax.rem(me + d, n)
        squares.append(
            send(square_out, square_landed.at[d - 1], "seq", peer, send_s.at[d - 1], recv_s.at[d - 1])
        )

    def pair(index):
        span = pl.ds(pl.multiple_of(index * units, units), units)
        gate = jnp.dot(mlp_in, wg_ref[:, span], preferred_element_type=jnp.float32)
        upward = jnp.dot(mlp_in, wu_ref[:, span], preferred_element_type=jnp.float32)
        return gate, upward

    pairs = []
    for d in range(1, n):
        peer = lax.rem(me + d, n)
        gate, upward = pair(peer)
        pair_out[d - 1, :, :units] = gate
        pair_out[d - 1, :, units:] = upward
        pairs.append(
            send(
                pair_out.at[d - 1],
                pair_landed.at[d - 1],
                "seq",
                peer,
                send_e.at[d - 1],
                recv_e.at[d - 1],
            )
        )
    gate, upward = pair(me)
    for copy in squares:
        copy.wait()
    square_sum = square_out[...]
    for d in range(1, n):
        square_sum = square_sum + square_landed[d - 1]
    column = lax.dot_general(
        square_sum,
        jnp.full((8, units), 0.125, jnp.float32),
        (((0,), (0,)), ((), ())),
        precision=lax.Precision.HIGHEST,
        preferred_element_type=jnp.float32,
    )
    inv_mid = lax.rsqrt(column / D + EPSILON)
    for d in range(1, n):
        pairs[d - 1].wait_recv()
        gate = gate + pair_landed[d - 1, :, :units]
        upward = upward + pair_landed[d - 1, :, units:]
    gate = gate * inv_mid
    act = (gate / (1.0 + jnp.exp(-gate)) * (upward * inv_mid)).astype(jnp.bfloat16)
    acts[0] = act
    activated = []
    for d in range(1, n):
        peer = lax.rem(me + d, n)
        activated.append(
            send(acts.at[0], acts.at[d], "seq", peer, send_f.at[d - 1], recv_f.at[d - 1])
        )

    def down(slot, index):
        span = pl.ds(pl.multiple_of(index * units, units), units)
        return jnp.dot(acts[slot], wd_ref[span, :], preferred_element_type=jnp.float32)

    product = down(0, me)
    for copy in pairs:
        copy.wait_send()
    for d in range(1, n):
        activated[d - 1].wait_recv()
        product = product + down(d, lax.rem(me + n - d, n))
    flat[...] = product
    for copy in activated:
        copy.wait_send()
    last[rank] = (mid_own + tp_scatter(down_landed, send_g, recv_g)).astype(jnp.bfloat16)
    tp_gather(last, send_h, recv_h)
    out_ref[...] = last[...]


def fused_body(
    n,
    m,
    hidden_in,
    attn_gain,
    w_query,
    w_key,
    w_value,
    w_out,
    mlp_gain,
    w_gate,
    w_up,
    w_down,
    kv_pages,
    lengths,
    group_ids,
    shared_table,
    own_table,
):
    seq_index = lax.axis_index("seq")
    steps, requests, local_width = hidden_in.shape
    cols = w_query.shape[1]
    flat_rows = steps * requests
    rows = flat_rows // n
    padded = -(-rows // 16) * 16
    group = flat_rows // m
    units = w_gate.shape[1] // n
    page_rows = kv_pages.shape[2]
    local_pages = own_table.shape[1]
    block_len = local_pages * page_rows
    group_count, prompt_pages = shared_table.shape
    f32, bf16 = jnp.float32, jnp.bfloat16

    logical = seq_index * local_pages + jnp.arange(local_pages, dtype=jnp.int32)
    group_pick = (group_ids[:, None] == jnp.arange(group_count, dtype=jnp.int32)[None, :]).astype(
        jnp.int32
    )
    group_rows = jnp.sum(group_pick[:, :, None] * shared_table[None, :, :], axis=1)
    column_pick = (logical[:, None] == jnp.arange(prompt_pages, dtype=jnp.int32)[None, :]).astype(
        jnp.int32
    )
    shared_local = jnp.sum(group_rows[:, None, :] * column_pick[None, :, :], axis=2)
    physical = jnp.where(logical[None, :] < prompt_pages, shared_local, own_table)

    x = jnp.transpose(hidden_in, (1, 0, 2)).reshape(flat_rows, local_width)
    halfway = HEAD_DIM // 2
    frequency = ROPE_BASE ** (-(jnp.arange(halfway, dtype=f32) * 2.0 / HEAD_DIM))
    where_now = (lengths[:, None] + jnp.arange(steps, dtype=jnp.int32)[None, :]).reshape(-1)
    angles = where_now[:, None].astype(f32) * frequency
    cosine = jnp.tile(jnp.cos(angles), (1, cols // halfway)).reshape(n, rows, cols)
    sine = jnp.tile(jnp.sin(angles), (1, cols // halfway)).reshape(n, rows, cols)

    vmem = pl.BlockSpec(memory_space=pltpu.VMEM)
    smem = pl.BlockSpec(memory_space=pltpu.SMEM)
    dma = pltpu.SemaphoreType.DMA
    wide = 3 * cols
    qkv = pl.pallas_call(
        functools.partial(project_kernel, n),
        out_shape=jax.ShapeDtypeStruct((requests, steps, wide), f32),
        in_specs=[vmem] * 7,
        out_specs=vmem,
        scratch_shapes=[
            pltpu.VMEM((flat_rows, wide + LANES), f32),
            pltpu.VMEM((n, rows, wide + LANES), f32),
            pltpu.VMEM((n - 1, rows, wide + LANES), f32),
            pltpu.VMEM((n, padded, wide), bf16),
        ]
        + [dma((n - 1,))] * 4,
        compiler_params=pltpu.CompilerParams(
            collective_id=0, has_side_effects=True, vmem_limit_bytes=48 << 20
        ),
    )(x, attn_gain.reshape(1, -1), w_query, w_key, w_value, cosine, sine)
    new_cache = jnp.transpose(
        qkv[:, :, cols:].astype(bf16).reshape(requests, steps, 2, cols), (2, 1, 0, 3)
    )

    attended = pl.pallas_call(
        attend_kernel,
        out_shape=jax.ShapeDtypeStruct((requests, steps, cols + LANES), f32),
        in_specs=[smem, smem, vmem, pl.BlockSpec(memory_space=pl.ANY)],
        out_specs=vmem,
        scratch_shapes=[
            pltpu.VMEM((requests, 2, block_len, cols), bf16),
            dma((requests, local_pages)),
        ],
        compiler_params=pltpu.CompilerParams(vmem_limit_bytes=48 << 20),
    )(lengths, physical, qkv, kv_pages)

    result = pl.pallas_call(
        functools.partial(finish_kernel, n, m),
        out_shape=jax.ShapeDtypeStruct((m, group, local_width), bf16),
        in_specs=[vmem] * 7,
        out_specs=vmem,
        scratch_shapes=[
            pltpu.VMEM((n, rows, cols + LANES), f32),
            pltpu.VMEM((n - 1, rows, cols + LANES), f32),
            pltpu.VMEM((n, padded, cols), bf16),
            pltpu.VMEM((flat_rows, local_width), f32),
            pltpu.VMEM((m - 1, group, local_width), f32),
            pltpu.VMEM((m, group, local_width), f32),
            pltpu.VMEM((n - 1, flat_rows, 2 * units), f32),
            pltpu.VMEM((n - 1, flat_rows, 2 * units), f32),
            pltpu.VMEM((8, flat_rows), f32),
            pltpu.VMEM((n - 1, 8, flat_rows), f32),
            pltpu.VMEM((n, flat_rows, units), bf16),
            pltpu.VMEM((m - 1, group, local_width), f32),
            pltpu.VMEM((m, group, local_width), bf16),
        ]
        + [dma((n - 1,))] * 4
        + [dma((m - 1,))] * 4
        + [dma((n - 1,))] * 6
        + [dma((m - 1,))] * 4,
        compiler_params=pltpu.CompilerParams(
            collective_id=1, has_side_effects=True, vmem_limit_bytes=48 << 20
        ),
    )(attended, x.astype(f32), mlp_gain.reshape(1, -1), w_out, w_gate, w_up, w_down)
    hidden_out = jnp.transpose(result.reshape(requests, steps, local_width), (1, 0, 2))
    return (hidden_out, new_cache)


def fits(n, m):
    flat_rows = 96
    return (
        n > 1
        and m > 1
        and flat_rows % (n * 4) == 0
        and flat_rows % (m * 8) == 0
        and D // m % LANES == 0
        and D // m // HEAD_DIM <= 8
    )


def solution(mesh):
    n, m = mesh.shape["seq"], mesh.shape["tp"]
    chosen = functools.partial(fused_body, n, m) if fits(n, m) else body
    return jax.shard_map(
        chosen,
        mesh=mesh,
        in_specs=(
            P(None, None, "seq"),
            P("seq"),
            P("seq", "tp"),
            P("seq", "tp"),
            P("seq", "tp"),
            P("tp", "seq"),
            P("seq"),
            P("seq", "tp"),
            P("seq", "tp"),
            P("tp", "seq"),
            P(None, "seq", None, "tp"),
            P(),
            P(),
            P(),
            P(None, "seq"),
        ),
        out_specs=(P(None, None, "seq"), P(None, None, None, "tp")),
        check_vma=False,
    )
```

```python
import functools
import math

import jax
import jax.numpy as jnp
from jax import lax
from jax.experimental import pallas as pl
from jax.experimental.pallas import tpu as pltpu
from jax.sharding import PartitionSpec as P

D = 3072
HEAD_DIM = 96
SINKS = 4
WINDOW = 1024


EPSILON = 1e-05
ROPE_BASE = 10000.0
NEGATIVE = -1e30


def rotate(vector, position):
    halfway = vector.shape[-1] // 2
    frequency = ROPE_BASE ** (-(jnp.arange(halfway, dtype=jnp.float32) * 2.0 / vector.shape[-1]))
    angles = position[..., None].astype(jnp.float32) * frequency
    cosine = jnp.cos(angles)
    sine_part = jnp.sin(angles)
    first_half = vector[..., :halfway]
    second_half = vector[..., halfway:]
    return jnp.concatenate(
        [
            first_half * cosine - second_half * sine_part,
            second_half * cosine + first_half * sine_part,
        ],
        -1,
    )


def seq_total(partial_value, squares):
    return lax.psum((partial_value, squares), "seq")


def head_total(partial_value):
    return lax.psum(partial_value, "tp")


def body(
    hidden_in,
    attn_gain,
    w_query,
    w_key,
    w_value,
    w_out,
    mlp_gain,
    w_gate,
    w_up,
    w_down,
    kv_pages,
    lengths,
    group_ids,
    shared_table,
    own_table,
):
    seq_index = lax.axis_index("seq")
    step_count = hidden_in.shape[0]
    requests = hidden_in.shape[1]
    local_width = hidden_in.shape[2]
    head_cols = w_query.shape[1]
    local_heads = head_cols // HEAD_DIM
    unit_cols = w_gate.shape[1]
    page_rows = kv_pages.shape[2]
    local_pages = own_table.shape[1]
    block_len = local_pages * page_rows
    group_count = shared_table.shape[0]
    prompt_pages = shared_table.shape[1]
    score_scale = 1.0 / math.sqrt(HEAD_DIM)
    flat_rows = step_count * requests
    logical = seq_index * local_pages + jnp.arange(local_pages, dtype=jnp.int32)
    group_pick = (group_ids[:, None] == jnp.arange(group_count, dtype=jnp.int32)[None, :]).astype(
        jnp.int32
    )
    group_rows = jnp.sum(group_pick[:, :, None] * shared_table[None, :, :], axis=1)
    column_pick = (logical[:, None] == jnp.arange(prompt_pages, dtype=jnp.int32)[None, :]).astype(
        jnp.int32
    )
    shared_local = jnp.sum(group_rows[:, None, :] * column_pick[None, :, :], axis=2)
    physical = jnp.where(logical[None, :] < prompt_pages, shared_local, own_table)
    gathered = kv_pages[:, physical]
    cached_keys = gathered[0].reshape(requests, block_len, local_heads, HEAD_DIM)
    cached_values = (
        gathered[1].reshape(requests, block_len, local_heads, HEAD_DIM).astype(jnp.float32)
    )
    positions = seq_index * block_len + jnp.arange(block_len, dtype=jnp.int32)
    step_ids = jnp.arange(step_count, dtype=jnp.int32)
    owner_new = jnp.transpose((lengths[None, :] + step_ids[:, None]) // block_len == seq_index)
    attn_scale = attn_gain.astype(jnp.float32)
    mlp_scale = mlp_gain.astype(jnp.float32)
    w_pair = jnp.concatenate([w_gate, w_up], axis=1)
    residual = hidden_in.astype(jnp.float32).reshape(flat_rows, local_width)
    normed = (residual * attn_scale).astype(jnp.bfloat16)
    squares = jnp.sum(residual * residual, axis=-1)
    where_now = lengths[None, :] + step_ids[:, None]
    w_qkv = jnp.concatenate([w_query, w_key, w_value], axis=1)
    partial_value = jnp.dot(normed, w_qkv, preferred_element_type=jnp.float32)
    summed, square_sum = seq_total(partial_value, squares)
    inv_rms = lax.rsqrt(square_sum / D + EPSILON)
    projected = (summed * inv_rms[:, None]).reshape(step_count, requests, 3, local_heads, HEAD_DIM)
    queries = rotate(projected[:, :, 0], where_now[:, :, None]).astype(jnp.bfloat16)
    key_new = (
        rotate(projected[:, :, 1], where_now[:, :, None])
        .astype(jnp.bfloat16)
        .reshape(step_count, requests, head_cols)
    )
    value_new = projected[:, :, 2].astype(jnp.bfloat16).reshape(step_count, requests, head_cols)
    store_keys = key_new.reshape(step_count, requests, local_heads, HEAD_DIM)
    store_values = value_new.reshape(step_count, requests, local_heads, HEAD_DIM).astype(
        jnp.float32
    )
    in_window = positions[None, None, :] > lengths[None, :, None] + step_ids[:, None, None] - WINDOW
    is_live = (positions[None, None, :] < lengths[None, :, None]) & (
        (positions[None, None, :] < SINKS) | in_window
    )
    new_live = (step_ids[None, None, :] <= step_ids[:, None, None]) & owner_new[None, :, :]
    scores = (
        jnp.einsum("tbhd,bkhd->tbhk", queries, cached_keys, preferred_element_type=jnp.float32)
        * score_scale
    )
    new_scores = (
        jnp.einsum("tbhd,sbhd->tbhs", queries, store_keys, preferred_element_type=jnp.float32)
        * score_scale
    )
    scores = jnp.where(is_live[:, :, None, :], scores, NEGATIVE)
    new_scores = jnp.where(new_live[:, :, None, :], new_scores, NEGATIVE)
    local_peak = jnp.maximum(jnp.max(scores, axis=-1), jnp.max(new_scores, axis=-1))
    score_peak = lax.pmax(local_peak, "seq")
    weights = jnp.where(is_live[:, :, None, :], jnp.exp(scores - score_peak[..., None]), 0.0)
    new_weights = jnp.where(
        new_live[:, :, None, :], jnp.exp(new_scores - score_peak[..., None]), 0.0
    )
    weight_sum = jnp.sum(weights, axis=-1) + jnp.sum(new_weights, axis=-1)
    weighted = jnp.einsum("tbhk,bkhd->tbhd", weights, cached_values) + jnp.einsum(
        "tbhs,sbhd->tbhd", new_weights, store_values
    )
    local_sum = weight_sum
    local_weighted = weighted
    weight_sum, weighted = lax.psum((local_sum, local_weighted), "seq")
    attn = (weighted / weight_sum[..., None]).astype(jnp.bfloat16).reshape(flat_rows, head_cols)
    mid_rows = residual + head_total(jnp.dot(attn, w_out, preferred_element_type=jnp.float32))
    mlp_in = (mid_rows * mlp_scale).astype(jnp.bfloat16)
    mid_squares = jnp.sum(mid_rows * mid_rows, axis=-1)
    gate_up = jnp.dot(mlp_in, w_pair, preferred_element_type=jnp.float32)
    pair_sum, mid_sum = seq_total(gate_up, mid_squares)
    inv_mid = lax.rsqrt(mid_sum / D + EPSILON)[:, None]
    activated = (
        jax.nn.silu(pair_sum[:, :unit_cols] * inv_mid) * (pair_sum[:, unit_cols:] * inv_mid)
    ).astype(jnp.bfloat16)
    result = (
        mid_rows + head_total(jnp.dot(activated, w_down, preferred_element_type=jnp.float32))
    ).astype(jnp.bfloat16)
    hidden_out = result.reshape(step_count, requests, local_width)
    return (hidden_out, jnp.stack([key_new, value_new]))


MESH_ID = pl.DeviceIdType.MESH
LANES = 128
HALF_LANES = 64


def greet(axes):
    barrier = pltpu.get_barrier_semaphore()
    total = 0
    for axis, size in axes:
        me = lax.axis_index(axis)
        for step in range(1, size):
            pl.semaphore_signal(
                barrier,
                inc=1,
                device_id={axis: lax.rem(me + step, size)},
                device_id_type=MESH_ID,
            )
            total += 1
    pl.semaphore_wait(barrier, total)


def send(source, target, axis, peer, send_sem, recv_sem):
    copy = pltpu.make_async_remote_copy(
        src_ref=source,
        dst_ref=target,
        send_sem=send_sem,
        recv_sem=recv_sem,
        device_id={axis: peer},
        device_id_type=MESH_ID,
    )
    copy.start()
    return copy


def place_of(n):
    me = lax.axis_index("seq")
    near = lax.rem(me, 2)
    far = me // 2
    half = n // 2

    def device(step, other):
        side = 1 - near if other else near
        return 2 * lax.rem(far + step + half, half) + side

    return me, half, device


def pair_scatter(n, make, put, get, near_out, near_in, far_out, far_in, sems):
    me, half, device = place_of(n)
    partner = device(0, True)
    near_send, near_recv, far_send, far_recv = sems
    order = list(range(1, half)) + [0]
    near = {}
    for d in order:
        put(near_out, d, make(device(d, True)))
        near[d] = send(
            near_out.at[d], near_in.at[d], "seq", partner, near_send.at[d], near_recv.at[d]
        )
    far = {}
    for d in range(1, half):
        peer = device(d, False)
        value = make(peer)
        near[d].wait_recv()
        put(far_out, d - 1, value + get(near_in, d))
        far[d] = send(
            far_out.at[d - 1], far_in.at[d - 1], "seq", peer, far_send.at[d - 1], far_recv.at[d - 1]
        )
    total = make(me)
    near[0].wait_recv()
    total = total + get(near_in, 0)
    for d in range(1, half):
        far[d].wait_recv()
        total = total + get(far_in, d - 1)
    return total, list(near.values()) + list(far.values())


def pair_gather(n, buffer, sems, arrive):
    me, half, device = place_of(n)
    partner = device(0, True)
    near_send, near_recv, far_send, far_recv = sems

    def share(index, peer, send_sem, recv_sem):
        return send(buffer.at[index], buffer.at[index], "seq", peer, send_sem, recv_sem)

    far = {}
    near = {}
    for d in range(1, half):
        far[d] = share(me, device(d, False), far_send.at[d - 1], far_recv.at[d - 1])
    near[0] = share(me, partner, near_send.at[0], near_recv.at[0])
    arrive(me)
    for d in range(1, half):
        far[d].wait_recv()
        index = device(-d, False)
        near[d] = share(index, partner, near_send.at[d], near_recv.at[d])
        arrive(index)
    for d in range(half):
        near[d].wait_recv()
        arrive(device(-d, True))
    return list(near.values()) + list(far.values())


def packed_width(width):
    return width + -(-width // (2 * LANES)) * LANES


def put_rows(ref, slot, value):
    width = value.shape[1]
    first = packed_width(width) - width
    ref[slot, :, :width] = value[:8]
    ref[slot, 0:4, width:] = value[8:12, :first]
    ref[slot, 4:8, width : 2 * width - first] = value[8:12, first:]
    if 2 * first > width:
        ref[slot, 4:8, 2 * width - first :] = jnp.zeros((4, 2 * first - width), value.dtype)


def get_rows(ref, slot, width):
    first = packed_width(width) - width
    value = ref[slot]
    rest = jnp.concatenate(
        [value[0:4, width:], value[4:8, width : 2 * width - first]], axis=1
    )
    return jnp.concatenate([value[:, :width], rest], axis=0)


def project_kernel(
    n,
    x_ref,
    gain_ref,
    wq_ref,
    wk_ref,
    wv_ref,
    cos_ref,
    sin_ref,
    out_ref,
    partial,
    near_out,
    near_in,
    far_out,
    far_in,
    shared,
    *sems,
):
    me = lax.axis_index("seq")
    cols = wq_ref.shape[1]
    width = 3 * cols
    steps = out_ref.shape[1]
    rows = cos_ref.shape[1]
    x = x_ref[...].astype(jnp.float32)
    normed = (x * gain_ref[...].astype(jnp.float32)).astype(jnp.bfloat16)
    squares = jnp.sum(x * x, axis=-1, keepdims=True)

    def store(value, first, last):
        for j in range(n):
            partial[j, :, first:last] = value[j * rows : (j + 1) * rows]

    for index, weight in enumerate((wq_ref, wk_ref, wv_ref)):
        store(
            jnp.dot(normed, weight[...], preferred_element_type=jnp.float32),
            index * cols,
            (index + 1) * cols,
        )
    store(jnp.broadcast_to(squares, (x.shape[0], LANES)), width, width + LANES)
    greet((("seq", n),))
    total, copies = pair_scatter(
        n,
        lambda index: partial[index],
        put_rows,
        lambda ref, slot: get_rows(ref, slot, width + LANES),
        near_out,
        near_in,
        far_out,
        far_in,
        sems[:4],
    )
    inv_rms = lax.rsqrt(total[:, width : width + 1] / D + EPSILON)
    projected = total[:, :width] * inv_rms
    lane = lax.broadcasted_iota(jnp.int32, (rows, cols), 1)
    early = lax.rem(lane, HEAD_DIM) < HEAD_DIM // 2
    cosine = cos_ref[me]
    sine = sin_ref[me]

    def turn(vector):
        ahead = pltpu.roll(vector, cols - HEAD_DIM // 2, 1)
        behind = pltpu.roll(vector, HEAD_DIM // 2, 1)
        return vector * cosine + jnp.where(early, -ahead, behind) * sine

    ready = jnp.concatenate(
        [
            turn(projected[:, :cols]),
            turn(projected[:, cols : 2 * cols]),
            projected[:, 2 * cols :],
        ],
        axis=1,
    )
    shared[me] = jnp.concatenate(
        [ready, jnp.zeros((shared.shape[1] - rows, width), jnp.float32)], axis=0
    ).astype(jnp.bfloat16)

    def arrive(index):
        held = shared[index].astype(jnp.float32)
        for i in range(rows // steps):
            out_ref[index * (rows // steps) + i] = held[i * steps : (i + 1) * steps]

    copies += pair_gather(n, shared, sems[4:], arrive)
    for copy in copies:
        copy.wait_send()


def attend_kernel(
    lengths_ref, pages_ref, qkv_ref, kv_ref, out_ref, pages, page_sem
):
    seq_index = lax.axis_index("seq")
    requests, steps = qkv_ref.shape[0], qkv_ref.shape[1]
    cols = pages.shape[-1]
    block_len = pages.shape[2]
    local_pages = page_sem.shape[1]
    page_rows = block_len // local_pages
    heads = cols // HEAD_DIM
    base = seq_index * block_len
    scale = 1.0 / math.sqrt(HEAD_DIM)

    def page_copy(b, p):
        return pltpu.make_async_copy(
            kv_ref.at[:, pages_ref[b, p]],
            pages.at[b, :, pl.ds(p * page_rows, page_rows)],
            page_sem.at[b, p],
        )

    def is_used(b):
        length = lengths_ref[b]
        return (base < length + steps) & ((base < SINKS) | (base + block_len > length - WINDOW))

    @pl.loop(0, requests)
    def _(b):
        @pl.when(is_used(b))
        def _():
            for p in range(local_pages):
                page_copy(b, p).start()

    head_row = lax.broadcasted_iota(jnp.int32, (heads, cols), 0) * HEAD_DIM
    head_lane = lax.broadcasted_iota(jnp.int32, (heads, cols), 1)
    own = jnp.where((head_lane >= head_row) & (head_lane < head_row + HEAD_DIM), 1.0, 0.0)
    stat_lane = lax.broadcasted_iota(jnp.int32, (heads, LANES), 1)
    stat_row = lax.broadcasted_iota(jnp.int32, (heads, LANES), 0)
    pick_peak = jnp.where(stat_lane == stat_row, 1.0, 0.0)
    pick_sum = jnp.where(stat_lane == stat_row + HALF_LANES, 1.0, 0.0)
    row_step = lax.broadcasted_iota(jnp.int32, (steps * heads, block_len), 0) // heads
    place = base + lax.broadcasted_iota(jnp.int32, (steps * heads, block_len), 1)
    page_row = lax.broadcasted_iota(jnp.int32, (page_rows, cols), 0)
    idle_lane = lax.broadcasted_iota(jnp.int32, (steps, cols + LANES), 1)
    idle = jnp.where((idle_lane >= cols) & (idle_lane < cols + HALF_LANES), NEGATIVE, 0.0)

    together = 4

    @pl.loop(0, requests // together)
    def _(block):
        for k in range(together):
            b = block * together + k

            @pl.when(is_used(b))
            def _():
                length = lengths_ref[b]
                for p in range(local_pages):
                    page_copy(b, p).wait()
                for u in range(steps):
                    spot = length + u - base

                    @pl.when((spot >= 0) & (spot < block_len))
                    def _():
                        top = pl.multiple_of(spot // page_rows * page_rows, page_rows)
                        hit = page_row == spot - top
                        for kind in range(2):
                            fresh = qkv_ref[b, u : u + 1, (kind + 1) * cols : (kind + 2) * cols]
                            old = pages[b, kind, pl.ds(top, page_rows), :].astype(jnp.float32)
                            pages[b, kind, pl.ds(top, page_rows), :] = jnp.where(
                                hit, fresh, old
                            ).astype(jnp.bfloat16)

        batch = [block * together + k for k in range(together)]
        all_scores = []
        for b in batch:
            wide = jnp.concatenate(
                [qkv_ref[b, t : t + 1, :cols] * own for t in range(steps)], axis=0
            ).astype(jnp.bfloat16)
            all_scores.append(
                lax.dot_general(
                    wide,
                    pages[b, 0],
                    (((1,), (1,)), ((), ())),
                    preferred_element_type=jnp.float32,
                )
                * scale
            )
        parts = []
        for b, scores in zip(batch, all_scores):
            reach = lengths_ref[b] + row_step
            live = (place <= reach) & ((place < SINKS) | (place > reach - WINDOW))
            scores = jnp.where(live, scores, NEGATIVE)
            peak = jnp.max(scores, axis=-1, keepdims=True)
            weights = jnp.where(live, jnp.exp(scores - peak), 0.0)
            weight_sum = jnp.sum(weights, axis=-1, keepdims=True)
            coarse = weights.astype(jnp.bfloat16)
            fine = (weights - coarse.astype(jnp.float32)).astype(jnp.bfloat16)
            parts.append((peak, weight_sum, jnp.concatenate([coarse, fine], axis=0)))
        for b, (peak, weight_sum, pieces) in zip(batch, parts):
            both = jnp.dot(pieces, pages[b, 1], preferred_element_type=jnp.float32)
            weighted = both[: steps * heads] + both[steps * heads :]
            used = is_used(b)
            for t in range(steps):
                part = slice(t * heads, (t + 1) * heads)
                row = jnp.sum(weighted[part] * own, axis=0, keepdims=True)
                stat = jnp.sum(
                    peak[part] * pick_peak + weight_sum[part] * pick_sum, axis=0, keepdims=True
                )
                out_ref[b, t : t + 1, :] = jnp.where(
                    used, jnp.concatenate([row, stat], axis=1), idle[t : t + 1]
                )


def finish_kernel(
    n,
    m,
    att_ref,
    x_ref,
    gain_ref,
    wo_ref,
    wg_ref,
    wu_ref,
    wd_ref,
    out_ref,
    chunks,
    landed,
    shared,
    flat,
    mid_landed,
    mid_all,
    near_out,
    near_in,
    far_out,
    far_in,
    square_out,
    square_landed,
    acts,
    down_landed,
    last,
    send_a,
    recv_a,
    send_s,
    recv_s,
    *sems,
):
    me = lax.axis_index("seq")
    rank = lax.axis_index("tp")
    tp_sems, seq_sems = sems[:8], sems[8:]
    steps = att_ref.shape[1]
    cols = wo_ref.shape[0]
    group = mid_all.shape[1]
    flat_rows = flat.shape[0]
    local_width = flat.shape[1]
    units = acts.shape[2]
    rows = flat_rows // n
    per = rows // steps
    for j in range(n):
        put_rows(chunks, j, jnp.concatenate([att_ref[j * per + i] for i in range(per)], axis=0))
    greet((("seq", n), ("tp", m)))
    copies = []
    for d in range(1, n):
        peer = lax.rem(me + d, n)
        copies.append(
            send(chunks.at[peer], landed.at[d - 1], "seq", peer, send_a.at[d - 1], recv_a.at[d - 1])
        )
    for copy in copies:
        copy.wait_recv()
    arrived = [get_rows(chunks, me, cols + LANES)] + [
        get_rows(landed, d - 1, cols + LANES) for d in range(1, n)
    ]
    stats = [value[:, cols:] for value in arrived]
    lane = lax.broadcasted_iota(jnp.int32, (rows, LANES), 1)
    is_peak = lane < HALF_LANES
    peaks = [jnp.where(is_peak, value, 0.0) for value in stats]
    top = functools.reduce(jnp.maximum, peaks)
    factors = [jnp.exp(value - top) for value in peaks]
    sums = [pltpu.roll(value, HALF_LANES, 1) for value in stats]
    total_sum = functools.reduce(lambda a, b: a + b, [f * s for f, s in zip(factors, sums)])
    heads = cols // HEAD_DIM
    inverse = 1.0 / jnp.where(lane < heads, total_sum, 1.0)
    spread_row = lax.broadcasted_iota(jnp.int32, (LANES, cols), 0) * HEAD_DIM
    spread_lane = lax.broadcasted_iota(jnp.int32, (LANES, cols), 1)
    spread = jnp.where(
        (spread_lane >= spread_row) & (spread_lane < spread_row + HEAD_DIM), 1.0, 0.0
    )
    attn = jnp.zeros((rows, cols), jnp.float32)
    for factor, value in zip(factors, arrived):
        share = jnp.where(lane < heads, factor * inverse, 0.0)
        attn = attn + value[:, :cols] * jnp.dot(
            share, spread, precision=lax.Precision.HIGHEST, preferred_element_type=jnp.float32
        )
    padded = shared.shape[1]
    shared[me] = jnp.concatenate(
        [attn, jnp.zeros((padded - rows, cols), jnp.float32)], axis=0
    ).astype(jnp.bfloat16)
    copies += pair_gather(n, shared, seq_sems[:4], lambda index: None)
    product = jnp.dot(
        shared[...].reshape(n * padded, cols), wo_ref[...], preferred_element_type=jnp.float32
    )
    for j in range(n):
        flat[j * rows : (j + 1) * rows, :] = product[j * padded : j * padded + rows]

    def tp_scatter(target, send_sem, recv_sem):
        started = []
        for d in range(1, m):
            peer = lax.rem(rank + d, m)
            first = pl.multiple_of(peer * group, group)
            started.append(
                send(
                    flat.at[pl.ds(first, group)],
                    target.at[d - 1],
                    "tp",
                    peer,
                    send_sem.at[d - 1],
                    recv_sem.at[d - 1],
                )
            )
        total = flat[pl.ds(pl.multiple_of(rank * group, group), group), :]
        for d in range(1, m):
            started[d - 1].wait_recv()
            total = total + target[d - 1]
        for copy in started:
            copy.wait_send()
        return total

    def tp_gather(buffer, send_sem, recv_sem):
        started = []
        for d in range(1, m):
            peer = lax.rem(rank + d, m)
            started.append(
                send(
                    buffer.at[rank],
                    buffer.at[rank],
                    "tp",
                    peer,
                    send_sem.at[d - 1],
                    recv_sem.at[d - 1],
                )
            )
        for copy in started:
            copy.wait()

    own_rows = pl.ds(pl.multiple_of(rank * group, group), group)
    mid_own = x_ref[own_rows, :] + tp_scatter(mid_landed, *tp_sems[0:2])
    mid_all[rank] = mid_own
    tp_gather(mid_all, *tp_sems[2:4])
    mid = mid_all[...].reshape(flat_rows, local_width)
    mlp_in = (mid * gain_ref[...].astype(jnp.float32)).astype(jnp.bfloat16)
    square_out[...] = lax.dot_general(
        jnp.ones((8, local_width), jnp.float32),
        mid * mid,
        (((1,), (1,)), ((), ())),
        precision=lax.Precision.HIGHEST,
        preferred_element_type=jnp.float32,
    )
    squares = []
    for d in range(1, n):
        peer = lax.rem(me + d, n)
        squares.append(
            send(square_out, square_landed.at[d - 1], "seq", peer, send_s.at[d - 1], recv_s.at[d - 1])
        )

    def pair(index):
        span = pl.ds(pl.multiple_of(index * units, units), units)
        return jnp.concatenate(
            [
                jnp.dot(mlp_in, wg_ref[:, span], preferred_element_type=jnp.float32),
                jnp.dot(mlp_in, wu_ref[:, span], preferred_element_type=jnp.float32),
            ],
            axis=1,
        )

    def put(ref, slot, value):
        ref[slot] = value.astype(ref.dtype)

    pair_total, pairs = pair_scatter(
        n,
        pair,
        put,
        lambda ref, slot: ref[slot].astype(jnp.float32),
        near_out,
        near_in,
        far_out,
        far_in,
        seq_sems[4:8],
    )
    copies += pairs
    for copy in squares:
        copy.wait()
    square_sum = square_out[...]
    for d in range(1, n):
        square_sum = square_sum + square_landed[d - 1]
    column = lax.dot_general(
        square_sum,
        jnp.full((8, units), 0.125, jnp.float32),
        (((0,), (0,)), ((), ())),
        precision=lax.Precision.HIGHEST,
        preferred_element_type=jnp.float32,
    )
    inv_mid = lax.rsqrt(column / D + EPSILON)
    gate = pair_total[:, :units] * inv_mid
    act = gate / (1.0 + jnp.exp(-gate)) * (pair_total[:, units:] * inv_mid)
    acts[me] = act.astype(jnp.bfloat16)
    flat[...] = jnp.zeros_like(flat)

    def down(index):
        span = pl.ds(pl.multiple_of(index * units, units), units)
        flat[...] += jnp.dot(acts[index], wd_ref[span, :], preferred_element_type=jnp.float32)

    copies += pair_gather(n, acts, seq_sems[8:12], down)
    for copy in copies:
        copy.wait_send()
    last[rank] = (mid_own + tp_scatter(down_landed, *tp_sems[4:6])).astype(jnp.bfloat16)
    tp_gather(last, *tp_sems[6:8])
    out_ref[...] = last[...]


def fused_body(
    n,
    m,
    hidden_in,
    attn_gain,
    w_query,
    w_key,
    w_value,
    w_out,
    mlp_gain,
    w_gate,
    w_up,
    w_down,
    kv_pages,
    lengths,
    group_ids,
    shared_table,
    own_table,
):
    seq_index = lax.axis_index("seq")
    steps, requests, local_width = hidden_in.shape
    cols = w_query.shape[1]
    flat_rows = steps * requests
    rows = flat_rows // n
    padded = -(-rows // 16) * 16
    group = flat_rows // m
    units = w_gate.shape[1] // n
    page_rows = kv_pages.shape[2]
    local_pages = own_table.shape[1]
    block_len = local_pages * page_rows
    group_count, prompt_pages = shared_table.shape
    f32, bf16 = jnp.float32, jnp.bfloat16

    logical = seq_index * local_pages + jnp.arange(local_pages, dtype=jnp.int32)
    group_pick = (group_ids[:, None] == jnp.arange(group_count, dtype=jnp.int32)[None, :]).astype(
        jnp.int32
    )
    group_rows = jnp.sum(group_pick[:, :, None] * shared_table[None, :, :], axis=1)
    column_pick = (logical[:, None] == jnp.arange(prompt_pages, dtype=jnp.int32)[None, :]).astype(
        jnp.int32
    )
    shared_local = jnp.sum(group_rows[:, None, :] * column_pick[None, :, :], axis=2)
    physical = jnp.where(logical[None, :] < prompt_pages, shared_local, own_table)

    x = jnp.transpose(hidden_in, (1, 0, 2)).reshape(flat_rows, local_width)
    halfway = HEAD_DIM // 2
    frequency = ROPE_BASE ** (-(jnp.arange(halfway, dtype=f32) * 2.0 / HEAD_DIM))
    where_now = (lengths[:, None] + jnp.arange(steps, dtype=jnp.int32)[None, :]).reshape(-1)
    angles = where_now[:, None].astype(f32) * frequency
    cosine = jnp.tile(jnp.cos(angles), (1, cols // halfway)).reshape(n, rows, cols)
    sine = jnp.tile(jnp.sin(angles), (1, cols // halfway)).reshape(n, rows, cols)

    vmem = pl.BlockSpec(memory_space=pltpu.VMEM)
    smem = pl.BlockSpec(memory_space=pltpu.SMEM)
    dma = pltpu.SemaphoreType.DMA
    wide = 3 * cols
    half = n // 2
    pair_sems = [dma((half,))] * 2 + [dma((half - 1,))] * 2
    qkv = pl.pallas_call(
        functools.partial(project_kernel, n),
        out_shape=jax.ShapeDtypeStruct((requests, steps, wide), f32),
        in_specs=[vmem] * 7,
        out_specs=vmem,
        scratch_shapes=[
            pltpu.VMEM((n, rows, wide + LANES), f32),
            pltpu.VMEM((half, 8, packed_width(wide + LANES)), f32),
            pltpu.VMEM((half, 8, packed_width(wide + LANES)), f32),
            pltpu.VMEM((half - 1, 8, packed_width(wide + LANES)), f32),
            pltpu.VMEM((half - 1, 8, packed_width(wide + LANES)), f32),
            pltpu.VMEM((n, padded, wide), bf16),
        ]
        + pair_sems * 2,
        compiler_params=pltpu.CompilerParams(
            collective_id=0, has_side_effects=True, vmem_limit_bytes=48 << 20
        ),
    )(x, attn_gain.reshape(1, -1), w_query, w_key, w_value, cosine, sine)
    new_cache = jnp.transpose(
        qkv[:, :, cols:].astype(bf16).reshape(requests, steps, 2, cols), (2, 1, 0, 3)
    )

    attended = pl.pallas_call(
        attend_kernel,
        out_shape=jax.ShapeDtypeStruct((requests, steps, cols + LANES), f32),
        in_specs=[smem, smem, vmem, pl.BlockSpec(memory_space=pl.ANY)],
        out_specs=vmem,
        scratch_shapes=[
            pltpu.VMEM((requests, 2, block_len, cols), bf16),
            dma((requests, local_pages)),
        ],
        compiler_params=pltpu.CompilerParams(vmem_limit_bytes=48 << 20),
    )(lengths, physical, qkv, kv_pages)

    result = pl.pallas_call(
        functools.partial(finish_kernel, n, m),
        out_shape=jax.ShapeDtypeStruct((m, group, local_width), bf16),
        in_specs=[vmem] * 7,
        out_specs=vmem,
        scratch_shapes=[
            pltpu.VMEM((n, 8, packed_width(cols + LANES)), f32),
            pltpu.VMEM((n - 1, 8, packed_width(cols + LANES)), f32),
            pltpu.VMEM((n, padded, cols), bf16),
            pltpu.VMEM((flat_rows, local_width), f32),
            pltpu.VMEM((m - 1, group, local_width), f32),
            pltpu.VMEM((m, group, local_width), f32),
            pltpu.VMEM((half, flat_rows, 2 * units), bf16),
            pltpu.VMEM((half, flat_rows, 2 * units), bf16),
            pltpu.VMEM((half - 1, flat_rows, 2 * units), bf16),
            pltpu.VMEM((half - 1, flat_rows, 2 * units), bf16),
            pltpu.VMEM((8, flat_rows), f32),
            pltpu.VMEM((n - 1, 8, flat_rows), f32),
            pltpu.VMEM((n, flat_rows, units), bf16),
            pltpu.VMEM((m - 1, group, local_width), f32),
            pltpu.VMEM((m, group, local_width), bf16),
        ]
        + [dma((n - 1,))] * 4
        + [dma((m - 1,))] * 8
        + pair_sems * 3,
        compiler_params=pltpu.CompilerParams(
            collective_id=1, has_side_effects=True, vmem_limit_bytes=48 << 20
        ),
    )(attended, x.astype(f32), mlp_gain.reshape(1, -1), w_out, w_gate, w_up, w_down)
    hidden_out = jnp.transpose(result.reshape(requests, steps, local_width), (1, 0, 2))
    return (hidden_out, new_cache)


def fits(n, m):
    flat_rows = 96
    return (
        n % 2 == 0
        and n > 2
        and m > 1
        and flat_rows == n * 12
        and flat_rows % (m * 8) == 0
        and D // m % LANES == 0
        and D // m // HEAD_DIM <= 8
    )


def solution(mesh):
    n, m = mesh.shape["seq"], mesh.shape["tp"]
    chosen = functools.partial(fused_body, n, m) if fits(n, m) else body
    return jax.shard_map(
        chosen,
        mesh=mesh,
        in_specs=(
            P(None, None, "seq"),
            P("seq"),
            P("seq", "tp"),
            P("seq", "tp"),
            P("seq", "tp"),
            P("tp", "seq"),
            P("seq"),
            P("seq", "tp"),
            P("seq", "tp"),
            P("tp", "seq"),
            P(None, "seq", None, "tp"),
            P(),
            P(),
            P(),
            P(None, "seq"),
        ),
        out_specs=(P(None, None, "seq"), P(None, None, None, "tp")),
        check_vma=False,
    )
```

```python
import functools
import math

import jax
import jax.numpy as jnp
from jax import lax
from jax.experimental import pallas as pl
from jax.experimental.pallas import tpu as pltpu
from jax.sharding import PartitionSpec as P

D = 3072
HEAD_DIM = 96
SINKS = 4
WINDOW = 1024


EPSILON = 1e-05
ROPE_BASE = 10000.0
NEGATIVE = -1e30


def rotate(vector, position):
    halfway = vector.shape[-1] // 2
    frequency = ROPE_BASE ** (-(jnp.arange(halfway, dtype=jnp.float32) * 2.0 / vector.shape[-1]))
    angles = position[..., None].astype(jnp.float32) * frequency
    cosine = jnp.cos(angles)
    sine_part = jnp.sin(angles)
    first_half = vector[..., :halfway]
    second_half = vector[..., halfway:]
    return jnp.concatenate(
        [
            first_half * cosine - second_half * sine_part,
            second_half * cosine + first_half * sine_part,
        ],
        -1,
    )


def seq_total(partial_value, squares):
    return lax.psum((partial_value, squares), "seq")


def head_total(partial_value):
    return lax.psum(partial_value, "tp")


def body(
    hidden_in,
    attn_gain,
    w_query,
    w_key,
    w_value,
    w_out,
    mlp_gain,
    w_gate,
    w_up,
    w_down,
    kv_pages,
    lengths,
    group_ids,
    shared_table,
    own_table,
):
    seq_index = lax.axis_index("seq")
    step_count = hidden_in.shape[0]
    requests = hidden_in.shape[1]
    local_width = hidden_in.shape[2]
    head_cols = w_query.shape[1]
    local_heads = head_cols // HEAD_DIM
    unit_cols = w_gate.shape[1]
    page_rows = kv_pages.shape[2]
    local_pages = own_table.shape[1]
    block_len = local_pages * page_rows
    group_count = shared_table.shape[0]
    prompt_pages = shared_table.shape[1]
    score_scale = 1.0 / math.sqrt(HEAD_DIM)
    flat_rows = step_count * requests
    logical = seq_index * local_pages + jnp.arange(local_pages, dtype=jnp.int32)
    group_pick = (group_ids[:, None] == jnp.arange(group_count, dtype=jnp.int32)[None, :]).astype(
        jnp.int32
    )
    group_rows = jnp.sum(group_pick[:, :, None] * shared_table[None, :, :], axis=1)
    column_pick = (logical[:, None] == jnp.arange(prompt_pages, dtype=jnp.int32)[None, :]).astype(
        jnp.int32
    )
    shared_local = jnp.sum(group_rows[:, None, :] * column_pick[None, :, :], axis=2)
    physical = jnp.where(logical[None, :] < prompt_pages, shared_local, own_table)
    gathered = kv_pages[:, physical]
    cached_keys = gathered[0].reshape(requests, block_len, local_heads, HEAD_DIM)
    cached_values = (
        gathered[1].reshape(requests, block_len, local_heads, HEAD_DIM).astype(jnp.float32)
    )
    positions = seq_index * block_len + jnp.arange(block_len, dtype=jnp.int32)
    step_ids = jnp.arange(step_count, dtype=jnp.int32)
    owner_new = jnp.transpose((lengths[None, :] + step_ids[:, None]) // block_len == seq_index)
    attn_scale = attn_gain.astype(jnp.float32)
    mlp_scale = mlp_gain.astype(jnp.float32)
    w_pair = jnp.concatenate([w_gate, w_up], axis=1)
    residual = hidden_in.astype(jnp.float32).reshape(flat_rows, local_width)
    normed = (residual * attn_scale).astype(jnp.bfloat16)
    squares = jnp.sum(residual * residual, axis=-1)
    where_now = lengths[None, :] + step_ids[:, None]
    w_qkv = jnp.concatenate([w_query, w_key, w_value], axis=1)
    partial_value = jnp.dot(normed, w_qkv, preferred_element_type=jnp.float32)
    summed, square_sum = seq_total(partial_value, squares)
    inv_rms = lax.rsqrt(square_sum / D + EPSILON)
    projected = (summed * inv_rms[:, None]).reshape(step_count, requests, 3, local_heads, HEAD_DIM)
    queries = rotate(projected[:, :, 0], where_now[:, :, None]).astype(jnp.bfloat16)
    key_new = (
        rotate(projected[:, :, 1], where_now[:, :, None])
        .astype(jnp.bfloat16)
        .reshape(step_count, requests, head_cols)
    )
    value_new = projected[:, :, 2].astype(jnp.bfloat16).reshape(step_count, requests, head_cols)
    store_keys = key_new.reshape(step_count, requests, local_heads, HEAD_DIM)
    store_values = value_new.reshape(step_count, requests, local_heads, HEAD_DIM).astype(
        jnp.float32
    )
    in_window = positions[None, None, :] > lengths[None, :, None] + step_ids[:, None, None] - WINDOW
    is_live = (positions[None, None, :] < lengths[None, :, None]) & (
        (positions[None, None, :] < SINKS) | in_window
    )
    new_live = (step_ids[None, None, :] <= step_ids[:, None, None]) & owner_new[None, :, :]
    scores = (
        jnp.einsum("tbhd,bkhd->tbhk", queries, cached_keys, preferred_element_type=jnp.float32)
        * score_scale
    )
    new_scores = (
        jnp.einsum("tbhd,sbhd->tbhs", queries, store_keys, preferred_element_type=jnp.float32)
        * score_scale
    )
    scores = jnp.where(is_live[:, :, None, :], scores, NEGATIVE)
    new_scores = jnp.where(new_live[:, :, None, :], new_scores, NEGATIVE)
    local_peak = jnp.maximum(jnp.max(scores, axis=-1), jnp.max(new_scores, axis=-1))
    score_peak = lax.pmax(local_peak, "seq")
    weights = jnp.where(is_live[:, :, None, :], jnp.exp(scores - score_peak[..., None]), 0.0)
    new_weights = jnp.where(
        new_live[:, :, None, :], jnp.exp(new_scores - score_peak[..., None]), 0.0
    )
    weight_sum = jnp.sum(weights, axis=-1) + jnp.sum(new_weights, axis=-1)
    weighted = jnp.einsum("tbhk,bkhd->tbhd", weights, cached_values) + jnp.einsum(
        "tbhs,sbhd->tbhd", new_weights, store_values
    )
    local_sum = weight_sum
    local_weighted = weighted
    weight_sum, weighted = lax.psum((local_sum, local_weighted), "seq")
    attn = (weighted / weight_sum[..., None]).astype(jnp.bfloat16).reshape(flat_rows, head_cols)
    mid_rows = residual + head_total(jnp.dot(attn, w_out, preferred_element_type=jnp.float32))
    mlp_in = (mid_rows * mlp_scale).astype(jnp.bfloat16)
    mid_squares = jnp.sum(mid_rows * mid_rows, axis=-1)
    gate_up = jnp.dot(mlp_in, w_pair, preferred_element_type=jnp.float32)
    pair_sum, mid_sum = seq_total(gate_up, mid_squares)
    inv_mid = lax.rsqrt(mid_sum / D + EPSILON)[:, None]
    activated = (
        jax.nn.silu(pair_sum[:, :unit_cols] * inv_mid) * (pair_sum[:, unit_cols:] * inv_mid)
    ).astype(jnp.bfloat16)
    result = (
        mid_rows + head_total(jnp.dot(activated, w_down, preferred_element_type=jnp.float32))
    ).astype(jnp.bfloat16)
    hidden_out = result.reshape(step_count, requests, local_width)
    return (hidden_out, jnp.stack([key_new, value_new]))


MESH_ID = pl.DeviceIdType.MESH
LANES = 128
HALF_LANES = 64


def greet(axes):
    barrier = pltpu.get_barrier_semaphore()
    total = 0
    for axis, size in axes:
        me = lax.axis_index(axis)
        for step in range(1, size):
            pl.semaphore_signal(
                barrier,
                inc=1,
                device_id={axis: lax.rem(me + step, size)},
                device_id_type=MESH_ID,
            )
            total += 1
    pl.semaphore_wait(barrier, total)


def send(source, target, axis, peer, send_sem, recv_sem):
    copy = pltpu.make_async_remote_copy(
        src_ref=source,
        dst_ref=target,
        send_sem=send_sem,
        recv_sem=recv_sem,
        device_id={axis: peer},
        device_id_type=MESH_ID,
    )
    copy.start()
    return copy


def place_of(n):
    me = lax.axis_index("seq")
    near = lax.rem(me, 2)
    far = me // 2
    half = n // 2

    def device(step, other):
        side = 1 - near if other else near
        return 2 * lax.rem(far + step + half, half) + side

    return me, half, device


def pair_scatter(n, make, put, get, near_out, near_in, far_out, far_in, sems):
    me, half, device = place_of(n)
    partner = device(0, True)
    near_send, near_recv, far_send, far_recv = sems
    order = list(range(1, half)) + [0]
    near = {}
    for d in order:
        put(near_out, d, make(device(d, True)))
        near[d] = send(
            near_out.at[d], near_in.at[d], "seq", partner, near_send.at[d], near_recv.at[d]
        )
    far = {}
    for d in range(1, half):
        peer = device(d, False)
        value = make(peer)
        near[d].wait_recv()
        put(far_out, d - 1, value + get(near_in, d))
        far[d] = send(
            far_out.at[d - 1], far_in.at[d - 1], "seq", peer, far_send.at[d - 1], far_recv.at[d - 1]
        )
    total = make(me)
    near[0].wait_recv()
    total = total + get(near_in, 0)
    for d in range(1, half):
        far[d].wait_recv()
        total = total + get(far_in, d - 1)
    return total, list(near.values()) + list(far.values())


def pair_gather(n, buffer, sems, arrive):
    me, half, device = place_of(n)
    partner = device(0, True)
    near_send, near_recv, far_send, far_recv = sems

    def share(index, peer, send_sem, recv_sem):
        return send(buffer.at[index], buffer.at[index], "seq", peer, send_sem, recv_sem)

    far = {}
    near = {}
    for d in range(1, half):
        far[d] = share(me, device(d, False), far_send.at[d - 1], far_recv.at[d - 1])
    near[0] = share(me, partner, near_send.at[0], near_recv.at[0])
    arrive(me)
    for d in range(1, half):
        far[d].wait_recv()
        index = device(-d, False)
        near[d] = share(index, partner, near_send.at[d], near_recv.at[d])
        arrive(index)
    for d in range(half):
        near[d].wait_recv()
        arrive(device(-d, True))
    return list(near.values()) + list(far.values())


def packed_width(width):
    return width + -(-width // (2 * LANES)) * LANES


def put_rows(ref, slot, value):
    width = value.shape[1]
    first = packed_width(width) - width
    ref[slot, :, :width] = value[:8]
    ref[slot, 0:4, width:] = value[8:12, :first]
    ref[slot, 4:8, width : 2 * width - first] = value[8:12, first:]
    if 2 * first > width:
        ref[slot, 4:8, 2 * width - first :] = jnp.zeros((4, 2 * first - width), value.dtype)


def get_rows(ref, slot, width):
    first = packed_width(width) - width
    value = ref[slot]
    rest = jnp.concatenate(
        [value[0:4, width:], value[4:8, width : 2 * width - first]], axis=1
    )
    return jnp.concatenate([value[:, :width], rest], axis=0)


def project_kernel(
    n,
    x_ref,
    gain_ref,
    wq_ref,
    wk_ref,
    wv_ref,
    cos_ref,
    sin_ref,
    out_ref,
    new_ref,
    partial,
    near_out,
    near_in,
    far_out,
    far_in,
    shared,
    *sems,
):
    me = lax.axis_index("seq")
    cols = wq_ref.shape[1]
    width = 3 * cols
    steps = out_ref.shape[1]
    rows = cos_ref.shape[1]
    x = x_ref[...].astype(jnp.float32)
    normed = (x * gain_ref[...].astype(jnp.float32)).astype(jnp.bfloat16)
    squares = jnp.sum(x * x, axis=-1, keepdims=True)

    def store(value, first, last):
        for j in range(n):
            partial[j, :, first:last] = value[j * rows : (j + 1) * rows]

    for index, weight in enumerate((wq_ref, wk_ref, wv_ref)):
        store(
            jnp.dot(normed, weight[...], preferred_element_type=jnp.float32),
            index * cols,
            (index + 1) * cols,
        )
    store(jnp.broadcast_to(squares, (x.shape[0], LANES)), width, width + LANES)
    greet((("seq", n),))
    total, copies = pair_scatter(
        n,
        lambda index: partial[index],
        put_rows,
        lambda ref, slot: get_rows(ref, slot, width + LANES),
        near_out,
        near_in,
        far_out,
        far_in,
        sems[:4],
    )
    inv_rms = lax.rsqrt(total[:, width : width + 1] / D + EPSILON)
    projected = total[:, :width] * inv_rms
    lane = lax.broadcasted_iota(jnp.int32, (rows, cols), 1)
    early = lax.rem(lane, HEAD_DIM) < HEAD_DIM // 2
    cosine = cos_ref[me]
    sine = sin_ref[me]

    def turn(vector):
        ahead = pltpu.roll(vector, cols - HEAD_DIM // 2, 1)
        behind = pltpu.roll(vector, HEAD_DIM // 2, 1)
        return vector * cosine + jnp.where(early, -ahead, behind) * sine

    spare = shared.shape[1] - rows

    def fill(value):
        return jnp.concatenate(
            [value, jnp.zeros((spare, value.shape[1]), jnp.float32)], axis=0
        ).astype(jnp.bfloat16)

    shared[me] = fill(turn(projected[:, :cols]))
    new_ref[:, :cols] = fill(turn(projected[:, cols : 2 * cols]))
    new_ref[:, cols:] = fill(projected[:, 2 * cols :])

    def arrive(index):
        held = shared[index].astype(jnp.float32)
        for i in range(rows // steps):
            out_ref[index * (rows // steps) + i] = held[i * steps : (i + 1) * steps]

    copies += pair_gather(n, shared, sems[4:], arrive)
    for copy in copies:
        copy.wait_send()


def head_masks(heads, cols):
    head_row = lax.broadcasted_iota(jnp.int32, (heads, cols), 0) * HEAD_DIM
    head_lane = lax.broadcasted_iota(jnp.int32, (heads, cols), 1)
    own = jnp.where((head_lane >= head_row) & (head_lane < head_row + HEAD_DIM), 1.0, 0.0)
    stat_lane = lax.broadcasted_iota(jnp.int32, (heads, LANES), 1)
    stat_row = lax.broadcasted_iota(jnp.int32, (heads, LANES), 0)
    pick_peak = jnp.where(stat_lane == stat_row, 1.0, 0.0)
    pick_sum = jnp.where(stat_lane == stat_row + HALF_LANES, 1.0, 0.0)
    return own, pick_peak, pick_sum


def attend_new(queries, keys, values, steps, heads):
    cols = queries[0].shape[1]
    own, pick_peak, pick_sum = head_masks(heads, cols)
    wide = jnp.concatenate(
        [value[t : t + 1] * own for value in queries for t in range(steps)], axis=0
    ).astype(jnp.bfloat16)
    scores = lax.dot_general(
        wide, keys, (((1,), (1,)), ((), ())), preferred_element_type=jnp.float32
    ) * (1.0 / math.sqrt(HEAD_DIM))
    query_row = lax.broadcasted_iota(jnp.int32, scores.shape, 0) // heads
    key_row = lax.broadcasted_iota(jnp.int32, scores.shape, 1)
    live = (key_row <= query_row) & (key_row // steps == query_row // steps)
    scores = jnp.where(live, scores, NEGATIVE)
    peak = jnp.max(scores, axis=-1, keepdims=True)
    weights = jnp.where(live, jnp.exp(scores - peak), 0.0)
    weight_sum = jnp.sum(weights, axis=-1, keepdims=True)
    coarse = weights.astype(jnp.bfloat16)
    fine = (weights - coarse.astype(jnp.float32)).astype(jnp.bfloat16)
    weighted = jnp.dot(coarse, values, preferred_element_type=jnp.float32) + jnp.dot(
        fine, values, preferred_element_type=jnp.float32
    )
    out = []
    for index in range(len(queries) * steps):
        part = slice(index * heads, (index + 1) * heads)
        out.append(
            jnp.concatenate(
                [
                    jnp.sum(weighted[part] * own, axis=0, keepdims=True),
                    jnp.sum(
                        peak[part] * pick_peak + weight_sum[part] * pick_sum,
                        axis=0,
                        keepdims=True,
                    ),
                ],
                axis=1,
            )
        )
    return jnp.concatenate(out, axis=0)


def attend_kernel(
    lengths_ref, pages_ref, query_ref, kv_ref, out_ref, pages, page_sem
):
    seq_index = lax.axis_index("seq")
    requests, steps = query_ref.shape[0], query_ref.shape[1]
    cols = pages.shape[-1]
    block_len = pages.shape[2]
    local_pages = page_sem.shape[1]
    page_rows = block_len // local_pages
    heads = cols // HEAD_DIM
    base = seq_index * block_len
    scale = 1.0 / math.sqrt(HEAD_DIM)

    def page_copy(b, p):
        return pltpu.make_async_copy(
            kv_ref.at[:, pages_ref[b, p]],
            pages.at[b, :, pl.ds(p * page_rows, page_rows)],
            page_sem.at[b, p],
        )

    def is_used(b):
        length = lengths_ref[b]
        return (base < length) & ((base < SINKS) | (base + block_len > length - WINDOW))

    @pl.loop(0, requests)
    def _(b):
        @pl.when(is_used(b))
        def _():
            for p in range(local_pages):
                page_copy(b, p).start()

    own, pick_peak, pick_sum = head_masks(heads, cols)
    row_step = lax.broadcasted_iota(jnp.int32, (steps * heads, block_len), 0) // heads
    place = base + lax.broadcasted_iota(jnp.int32, (steps * heads, block_len), 1)
    idle_lane = lax.broadcasted_iota(jnp.int32, (steps, cols + LANES), 1)
    idle = jnp.where((idle_lane >= cols) & (idle_lane < cols + HALF_LANES), NEGATIVE, 0.0)

    together = 4

    @pl.loop(0, requests // together)
    def _(block):
        for k in range(together):
            b = block * together + k

            @pl.when(is_used(b))
            def _():
                for p in range(local_pages):
                    page_copy(b, p).wait()

        batch = [block * together + k for k in range(together)]
        all_scores = []
        for b in batch:
            wide = jnp.concatenate(
                [query_ref[b, t : t + 1, :] * own for t in range(steps)], axis=0
            ).astype(jnp.bfloat16)
            all_scores.append(
                lax.dot_general(
                    wide,
                    pages[b, 0],
                    (((1,), (1,)), ((), ())),
                    preferred_element_type=jnp.float32,
                )
                * scale
            )
        parts = []
        for b, scores in zip(batch, all_scores):
            length = lengths_ref[b]
            live = (place < length) & ((place < SINKS) | (place > length + row_step - WINDOW))
            scores = jnp.where(live, scores, NEGATIVE)
            peak = jnp.max(scores, axis=-1, keepdims=True)
            weights = jnp.where(live, jnp.exp(scores - peak), 0.0)
            weight_sum = jnp.sum(weights, axis=-1, keepdims=True)
            coarse = weights.astype(jnp.bfloat16)
            fine = (weights - coarse.astype(jnp.float32)).astype(jnp.bfloat16)
            parts.append((peak, weight_sum, jnp.concatenate([coarse, fine], axis=0)))
        for b, (peak, weight_sum, pieces) in zip(batch, parts):
            both = jnp.dot(pieces, pages[b, 1], preferred_element_type=jnp.float32)
            weighted = both[: steps * heads] + both[steps * heads :]
            used = is_used(b)
            for t in range(steps):
                part = slice(t * heads, (t + 1) * heads)
                row = jnp.sum(weighted[part] * own, axis=0, keepdims=True)
                stat = jnp.sum(
                    peak[part] * pick_peak + weight_sum[part] * pick_sum, axis=0, keepdims=True
                )
                out_ref[b, t : t + 1, :] = jnp.where(
                    used, jnp.concatenate([row, stat], axis=1), idle[t : t + 1]
                )


def finish_kernel(
    n,
    m,
    att_ref,
    x_ref,
    gain_ref,
    wo_ref,
    wg_ref,
    wu_ref,
    wd_ref,
    query_ref,
    fresh_ref,
    out_ref,
    cache_ref,
    fresh_all,
    chunks,
    landed,
    shared,
    flat,
    mid_landed,
    mid_all,
    near_out,
    near_in,
    far_out,
    far_in,
    square_out,
    square_landed,
    acts,
    down_landed,
    last,
    send_a,
    recv_a,
    send_s,
    recv_s,
    *sems,
):
    me = lax.axis_index("seq")
    rank = lax.axis_index("tp")
    tp_sems, seq_sems = sems[:8], sems[8:]
    steps = att_ref.shape[1]
    cols = wo_ref.shape[0]
    group = mid_all.shape[1]
    flat_rows = flat.shape[0]
    local_width = flat.shape[1]
    units = acts.shape[2]
    rows = flat_rows // n
    per = rows // steps
    for j in range(n):
        put_rows(chunks, j, jnp.concatenate([att_ref[j * per + i] for i in range(per)], axis=0))
    greet((("seq", n), ("tp", m)))
    copies = []
    for d in range(1, n):
        peer = lax.rem(me + d, n)
        copies.append(
            send(chunks.at[peer], landed.at[d - 1], "seq", peer, send_a.at[d - 1], recv_a.at[d - 1])
        )
    heads = cols // HEAD_DIM
    fresh = attend_new(
        [query_ref[me * per + i] for i in range(per)],
        fresh_ref[:, :cols],
        fresh_ref[:, cols:],
        steps,
        heads,
    )
    fresh_all[me] = fresh_ref[...]
    for copy in copies:
        copy.wait_recv()
    arrived = [fresh, get_rows(chunks, me, cols + LANES)] + [
        get_rows(landed, d - 1, cols + LANES) for d in range(1, n)
    ]
    stats = [value[:, cols:] for value in arrived]
    lane = lax.broadcasted_iota(jnp.int32, (rows, LANES), 1)
    is_peak = lane < HALF_LANES
    peaks = [jnp.where(is_peak, value, 0.0) for value in stats]
    top = functools.reduce(jnp.maximum, peaks)
    factors = [jnp.exp(value - top) for value in peaks]
    sums = [pltpu.roll(value, HALF_LANES, 1) for value in stats]
    total_sum = functools.reduce(lambda a, b: a + b, [f * s for f, s in zip(factors, sums)])
    inverse = 1.0 / jnp.where(lane < heads, total_sum, 1.0)
    spread_row = lax.broadcasted_iota(jnp.int32, (LANES, cols), 0) * HEAD_DIM
    spread_lane = lax.broadcasted_iota(jnp.int32, (LANES, cols), 1)
    spread = jnp.where(
        (spread_lane >= spread_row) & (spread_lane < spread_row + HEAD_DIM), 1.0, 0.0
    ).astype(jnp.bfloat16)
    attn = jnp.zeros((rows, cols), jnp.float32)
    blank = jnp.zeros((16 - rows, LANES), jnp.float32)
    rest = jnp.concatenate(
        [
            jnp.concatenate([jnp.where(lane < heads, factor * inverse, 0.0), blank], axis=0)
            for factor in factors
        ],
        axis=0,
    )
    shares = 0.0
    for _ in range(3):
        piece = rest.astype(jnp.bfloat16)
        rest = rest - piece.astype(jnp.float32)
        shares = shares + jnp.dot(piece, spread, preferred_element_type=jnp.float32)
    for index, value in enumerate(arrived):
        attn = attn + value[:, :cols] * shares[index * 16 : index * 16 + rows]
    padded = shared.shape[1]
    shared[me] = jnp.concatenate(
        [attn, jnp.zeros((padded - rows, cols), jnp.float32)], axis=0
    ).astype(jnp.bfloat16)
    copies += pair_gather(n, shared, seq_sems[:4], lambda index: None)
    _, half, device = place_of(n)
    partner = device(0, True)
    near_send, near_recv, far_send, far_recv = seq_sems[12:16]

    def pass_on(index, peer, send_sem, recv_sem):
        return send(fresh_all.at[index], fresh_all.at[index], "seq", peer, send_sem, recv_sem)

    cache_far = {}
    for d in range(1, half):
        cache_far[d] = pass_on(me, device(d, False), far_send.at[d - 1], far_recv.at[d - 1])
    product = jnp.dot(
        shared[...].reshape(n * padded, cols), wo_ref[...], preferred_element_type=jnp.float32
    )
    for j in range(n):
        flat[j * rows : (j + 1) * rows, :] = product[j * padded : j * padded + rows]

    def tp_scatter(target, send_sem, recv_sem):
        started = []
        for d in range(1, m):
            peer = lax.rem(rank + d, m)
            first = pl.multiple_of(peer * group, group)
            started.append(
                send(
                    flat.at[pl.ds(first, group)],
                    target.at[d - 1],
                    "tp",
                    peer,
                    send_sem.at[d - 1],
                    recv_sem.at[d - 1],
                )
            )
        total = flat[pl.ds(pl.multiple_of(rank * group, group), group), :]
        for d in range(1, m):
            started[d - 1].wait_recv()
            total = total + target[d - 1]
        for copy in started:
            copy.wait_send()
        return total

    def tp_gather(buffer, send_sem, recv_sem):
        started = []
        for d in range(1, m):
            peer = lax.rem(rank + d, m)
            started.append(
                send(
                    buffer.at[rank],
                    buffer.at[rank],
                    "tp",
                    peer,
                    send_sem.at[d - 1],
                    recv_sem.at[d - 1],
                )
            )
        for copy in started:
            copy.wait()

    own_rows = pl.ds(pl.multiple_of(rank * group, group), group)
    mid_own = x_ref[own_rows, :] + tp_scatter(mid_landed, *tp_sems[0:2])
    mid_all[rank] = mid_own
    tp_gather(mid_all, *tp_sems[2:4])
    mid = mid_all[...].reshape(flat_rows, local_width)
    mlp_in = (mid * gain_ref[...].astype(jnp.float32)).astype(jnp.bfloat16)
    square_out[...] = lax.dot_general(
        jnp.ones((8, local_width), jnp.float32),
        mid * mid,
        (((1,), (1,)), ((), ())),
        precision=lax.Precision.HIGHEST,
        preferred_element_type=jnp.float32,
    )
    squares = []
    for d in range(1, n):
        peer = lax.rem(me + d, n)
        squares.append(
            send(square_out, square_landed.at[d - 1], "seq", peer, send_s.at[d - 1], recv_s.at[d - 1])
        )

    def pair(index):
        span = pl.ds(pl.multiple_of(index * units, units), units)
        return jnp.concatenate(
            [
                jnp.dot(mlp_in, wg_ref[:, span], preferred_element_type=jnp.float32),
                jnp.dot(mlp_in, wu_ref[:, span], preferred_element_type=jnp.float32),
            ],
            axis=1,
        )

    def put(ref, slot, value):
        ref[slot] = value.astype(ref.dtype)

    pair_total, pairs = pair_scatter(
        n,
        pair,
        put,
        lambda ref, slot: ref[slot].astype(jnp.float32),
        near_out,
        near_in,
        far_out,
        far_in,
        seq_sems[4:8],
    )
    copies += pairs
    for copy in squares:
        copy.wait()
    square_sum = square_out[...]
    for d in range(1, n):
        square_sum = square_sum + square_landed[d - 1]
    column = lax.dot_general(
        square_sum,
        jnp.full((8, units), 0.125, jnp.float32),
        (((0,), (0,)), ((), ())),
        precision=lax.Precision.HIGHEST,
        preferred_element_type=jnp.float32,
    )
    inv_mid = lax.rsqrt(column / D + EPSILON)
    gate = pair_total[:, :units] * inv_mid
    act = gate / (1.0 + jnp.exp(-gate)) * (pair_total[:, units:] * inv_mid)
    acts[me] = act.astype(jnp.bfloat16)
    flat[...] = jnp.zeros_like(flat)

    def down(index):
        span = pl.ds(pl.multiple_of(index * units, units), units)
        flat[...] += jnp.dot(acts[index], wd_ref[span, :], preferred_element_type=jnp.float32)

    copies += pair_gather(n, acts, seq_sems[8:12], down)
    for copy in copies:
        copy.wait_send()
    cache_near = [pass_on(me, partner, near_send.at[0], near_recv.at[0])]
    for d in range(1, half):
        cache_far[d].wait_recv()
        cache_near.append(
            pass_on(device(-d, False), partner, near_send.at[d], near_recv.at[d])
        )
    last[rank] = (mid_own + tp_scatter(down_landed, *tp_sems[4:6])).astype(jnp.bfloat16)
    tp_gather(last, *tp_sems[6:8])
    out_ref[...] = last[...]
    for copy in cache_near:
        copy.wait()
    for copy in cache_far.values():
        copy.wait_send()
    cache_ref[...] = fresh_all[...]


def fused_body(
    n,
    m,
    hidden_in,
    attn_gain,
    w_query,
    w_key,
    w_value,
    w_out,
    mlp_gain,
    w_gate,
    w_up,
    w_down,
    kv_pages,
    lengths,
    group_ids,
    shared_table,
    own_table,
):
    seq_index = lax.axis_index("seq")
    steps, requests, local_width = hidden_in.shape
    cols = w_query.shape[1]
    flat_rows = steps * requests
    rows = flat_rows // n
    padded = -(-rows // 16) * 16
    group = flat_rows // m
    units = w_gate.shape[1] // n
    page_rows = kv_pages.shape[2]
    local_pages = own_table.shape[1]
    block_len = local_pages * page_rows
    group_count, prompt_pages = shared_table.shape
    f32, bf16 = jnp.float32, jnp.bfloat16

    logical = seq_index * local_pages + jnp.arange(local_pages, dtype=jnp.int32)
    group_pick = (group_ids[:, None] == jnp.arange(group_count, dtype=jnp.int32)[None, :]).astype(
        jnp.int32
    )
    group_rows = jnp.sum(group_pick[:, :, None] * shared_table[None, :, :], axis=1)
    column_pick = (logical[:, None] == jnp.arange(prompt_pages, dtype=jnp.int32)[None, :]).astype(
        jnp.int32
    )
    shared_local = jnp.sum(group_rows[:, None, :] * column_pick[None, :, :], axis=2)
    physical = jnp.where(logical[None, :] < prompt_pages, shared_local, own_table)

    x = jnp.transpose(hidden_in, (1, 0, 2)).reshape(flat_rows, local_width)
    halfway = HEAD_DIM // 2
    frequency = ROPE_BASE ** (-(jnp.arange(halfway, dtype=f32) * 2.0 / HEAD_DIM))
    where_now = (lengths[:, None] + jnp.arange(steps, dtype=jnp.int32)[None, :]).reshape(-1)
    angles = where_now[:, None].astype(f32) * frequency
    cosine = jnp.tile(jnp.cos(angles), (1, cols // halfway)).reshape(n, rows, cols)
    sine = jnp.tile(jnp.sin(angles), (1, cols // halfway)).reshape(n, rows, cols)

    vmem = pl.BlockSpec(memory_space=pltpu.VMEM)
    smem = pl.BlockSpec(memory_space=pltpu.SMEM)
    dma = pltpu.SemaphoreType.DMA
    wide = 3 * cols
    half = n // 2
    pair_sems = [dma((half,))] * 2 + [dma((half - 1,))] * 2
    queries, fresh = pl.pallas_call(
        functools.partial(project_kernel, n),
        out_shape=(
            jax.ShapeDtypeStruct((requests, steps, cols), f32),
            jax.ShapeDtypeStruct((padded, 2 * cols), bf16),
        ),
        in_specs=[vmem] * 7,
        out_specs=(vmem, vmem),
        scratch_shapes=[
            pltpu.VMEM((n, rows, wide + LANES), f32),
            pltpu.VMEM((half, 8, packed_width(wide + LANES)), f32),
            pltpu.VMEM((half, 8, packed_width(wide + LANES)), f32),
            pltpu.VMEM((half - 1, 8, packed_width(wide + LANES)), f32),
            pltpu.VMEM((half - 1, 8, packed_width(wide + LANES)), f32),
            pltpu.VMEM((n, padded, cols), bf16),
        ]
        + pair_sems * 2,
        compiler_params=pltpu.CompilerParams(
            collective_id=0, has_side_effects=True, vmem_limit_bytes=48 << 20
        ),
    )(x, attn_gain.reshape(1, -1), w_query, w_key, w_value, cosine, sine)
    attended = pl.pallas_call(
        attend_kernel,
        out_shape=jax.ShapeDtypeStruct((requests, steps, cols + LANES), f32),
        in_specs=[smem, smem, vmem, pl.BlockSpec(memory_space=pl.ANY)],
        out_specs=vmem,
        scratch_shapes=[
            pltpu.VMEM((requests, 2, block_len, cols), bf16),
            dma((requests, local_pages)),
        ],
        compiler_params=pltpu.CompilerParams(vmem_limit_bytes=48 << 20),
    )(lengths, physical, queries, kv_pages)

    result, caches = pl.pallas_call(
        functools.partial(finish_kernel, n, m),
        out_shape=(
            jax.ShapeDtypeStruct((m, group, local_width), bf16),
            jax.ShapeDtypeStruct((n, padded, 2 * cols), bf16),
        ),
        in_specs=[vmem] * 9,
        out_specs=(vmem, vmem),
        scratch_shapes=[
            pltpu.VMEM((n, padded, 2 * cols), bf16),
            pltpu.VMEM((n, 8, packed_width(cols + LANES)), f32),
            pltpu.VMEM((n - 1, 8, packed_width(cols + LANES)), f32),
            pltpu.VMEM((n, padded, cols), bf16),
            pltpu.VMEM((flat_rows, local_width), f32),
            pltpu.VMEM((m - 1, group, local_width), f32),
            pltpu.VMEM((m, group, local_width), f32),
            pltpu.VMEM((half, flat_rows, 2 * units), bf16),
            pltpu.VMEM((half, flat_rows, 2 * units), bf16),
            pltpu.VMEM((half - 1, flat_rows, 2 * units), bf16),
            pltpu.VMEM((half - 1, flat_rows, 2 * units), bf16),
            pltpu.VMEM((8, flat_rows), f32),
            pltpu.VMEM((n - 1, 8, flat_rows), f32),
            pltpu.VMEM((n, flat_rows, units), bf16),
            pltpu.VMEM((m - 1, group, local_width), f32),
            pltpu.VMEM((m, group, local_width), bf16),
        ]
        + [dma((n - 1,))] * 4
        + [dma((m - 1,))] * 8
        + pair_sems * 4,
        compiler_params=pltpu.CompilerParams(
            collective_id=1, has_side_effects=True, vmem_limit_bytes=48 << 20
        ),
    )(
        attended,
        x.astype(f32),
        mlp_gain.reshape(1, -1),
        w_out,
        w_gate,
        w_up,
        w_down,
        queries,
        fresh,
    )
    new_cache = jnp.transpose(
        caches[:, :rows].reshape(requests, steps, 2, cols), (2, 1, 0, 3)
    )
    hidden_out = jnp.transpose(result.reshape(requests, steps, local_width), (1, 0, 2))
    return (hidden_out, new_cache)


def fits(n, m):
    flat_rows = 96
    return (
        n % 2 == 0
        and n > 2
        and m > 1
        and flat_rows == n * 12
        and flat_rows % (m * 8) == 0
        and D // m % LANES == 0
        and D // m // HEAD_DIM <= 8
    )


def solution(mesh):
    n, m = mesh.shape["seq"], mesh.shape["tp"]
    chosen = functools.partial(fused_body, n, m) if fits(n, m) else body
    return jax.shard_map(
        chosen,
        mesh=mesh,
        in_specs=(
            P(None, None, "seq"),
            P("seq"),
            P("seq", "tp"),
            P("seq", "tp"),
            P("seq", "tp"),
            P("tp", "seq"),
            P("seq"),
            P("seq", "tp"),
            P("seq", "tp"),
            P("tp", "seq"),
            P(None, "seq", None, "tp"),
            P(),
            P(),
            P(),
            P(None, "seq"),
        ),
        out_specs=(P(None, None, "seq"), P(None, None, None, "tp")),
        check_vma=False,
    )
```

```python
import functools
import math

import jax
import jax.numpy as jnp
from jax import lax
from jax.experimental import pallas as pl
from jax.experimental.pallas import tpu as pltpu
from jax.sharding import PartitionSpec as P

D = 3072
HEAD_DIM = 96
SINKS = 4
WINDOW = 1024


EPSILON = 1e-05
ROPE_BASE = 10000.0
NEGATIVE = -1e30


def rotate(vector, position):
    halfway = vector.shape[-1] // 2
    frequency = ROPE_BASE ** (-(jnp.arange(halfway, dtype=jnp.float32) * 2.0 / vector.shape[-1]))
    angles = position[..., None].astype(jnp.float32) * frequency
    cosine = jnp.cos(angles)
    sine_part = jnp.sin(angles)
    first_half = vector[..., :halfway]
    second_half = vector[..., halfway:]
    return jnp.concatenate(
        [
            first_half * cosine - second_half * sine_part,
            second_half * cosine + first_half * sine_part,
        ],
        -1,
    )


def seq_total(partial_value, squares):
    return lax.psum((partial_value, squares), "seq")


def head_total(partial_value):
    return lax.psum(partial_value, "tp")


def body(
    hidden_in,
    attn_gain,
    w_query,
    w_key,
    w_value,
    w_out,
    mlp_gain,
    w_gate,
    w_up,
    w_down,
    kv_pages,
    lengths,
    group_ids,
    shared_table,
    own_table,
):
    seq_index = lax.axis_index("seq")
    step_count = hidden_in.shape[0]
    requests = hidden_in.shape[1]
    local_width = hidden_in.shape[2]
    head_cols = w_query.shape[1]
    local_heads = head_cols // HEAD_DIM
    unit_cols = w_gate.shape[1]
    page_rows = kv_pages.shape[2]
    local_pages = own_table.shape[1]
    block_len = local_pages * page_rows
    group_count = shared_table.shape[0]
    prompt_pages = shared_table.shape[1]
    score_scale = 1.0 / math.sqrt(HEAD_DIM)
    flat_rows = step_count * requests
    logical = seq_index * local_pages + jnp.arange(local_pages, dtype=jnp.int32)
    group_pick = (group_ids[:, None] == jnp.arange(group_count, dtype=jnp.int32)[None, :]).astype(
        jnp.int32
    )
    group_rows = jnp.sum(group_pick[:, :, None] * shared_table[None, :, :], axis=1)
    column_pick = (logical[:, None] == jnp.arange(prompt_pages, dtype=jnp.int32)[None, :]).astype(
        jnp.int32
    )
    shared_local = jnp.sum(group_rows[:, None, :] * column_pick[None, :, :], axis=2)
    physical = jnp.where(logical[None, :] < prompt_pages, shared_local, own_table)
    gathered = kv_pages[:, physical]
    cached_keys = gathered[0].reshape(requests, block_len, local_heads, HEAD_DIM)
    cached_values = (
        gathered[1].reshape(requests, block_len, local_heads, HEAD_DIM).astype(jnp.float32)
    )
    positions = seq_index * block_len + jnp.arange(block_len, dtype=jnp.int32)
    step_ids = jnp.arange(step_count, dtype=jnp.int32)
    owner_new = jnp.transpose((lengths[None, :] + step_ids[:, None]) // block_len == seq_index)
    attn_scale = attn_gain.astype(jnp.float32)
    mlp_scale = mlp_gain.astype(jnp.float32)
    w_pair = jnp.concatenate([w_gate, w_up], axis=1)
    residual = hidden_in.astype(jnp.float32).reshape(flat_rows, local_width)
    normed = (residual * attn_scale).astype(jnp.bfloat16)
    squares = jnp.sum(residual * residual, axis=-1)
    where_now = lengths[None, :] + step_ids[:, None]
    w_qkv = jnp.concatenate([w_query, w_key, w_value], axis=1)
    partial_value = jnp.dot(normed, w_qkv, preferred_element_type=jnp.float32)
    summed, square_sum = seq_total(partial_value, squares)
    inv_rms = lax.rsqrt(square_sum / D + EPSILON)
    projected = (summed * inv_rms[:, None]).reshape(step_count, requests, 3, local_heads, HEAD_DIM)
    queries = rotate(projected[:, :, 0], where_now[:, :, None]).astype(jnp.bfloat16)
    key_new = (
        rotate(projected[:, :, 1], where_now[:, :, None])
        .astype(jnp.bfloat16)
        .reshape(step_count, requests, head_cols)
    )
    value_new = projected[:, :, 2].astype(jnp.bfloat16).reshape(step_count, requests, head_cols)
    store_keys = key_new.reshape(step_count, requests, local_heads, HEAD_DIM)
    store_values = value_new.reshape(step_count, requests, local_heads, HEAD_DIM).astype(
        jnp.float32
    )
    in_window = positions[None, None, :] > lengths[None, :, None] + step_ids[:, None, None] - WINDOW
    is_live = (positions[None, None, :] < lengths[None, :, None]) & (
        (positions[None, None, :] < SINKS) | in_window
    )
    new_live = (step_ids[None, None, :] <= step_ids[:, None, None]) & owner_new[None, :, :]
    scores = (
        jnp.einsum("tbhd,bkhd->tbhk", queries, cached_keys, preferred_element_type=jnp.float32)
        * score_scale
    )
    new_scores = (
        jnp.einsum("tbhd,sbhd->tbhs", queries, store_keys, preferred_element_type=jnp.float32)
        * score_scale
    )
    scores = jnp.where(is_live[:, :, None, :], scores, NEGATIVE)
    new_scores = jnp.where(new_live[:, :, None, :], new_scores, NEGATIVE)
    local_peak = jnp.maximum(jnp.max(scores, axis=-1), jnp.max(new_scores, axis=-1))
    score_peak = lax.pmax(local_peak, "seq")
    weights = jnp.where(is_live[:, :, None, :], jnp.exp(scores - score_peak[..., None]), 0.0)
    new_weights = jnp.where(
        new_live[:, :, None, :], jnp.exp(new_scores - score_peak[..., None]), 0.0
    )
    weight_sum = jnp.sum(weights, axis=-1) + jnp.sum(new_weights, axis=-1)
    weighted = jnp.einsum("tbhk,bkhd->tbhd", weights, cached_values) + jnp.einsum(
        "tbhs,sbhd->tbhd", new_weights, store_values
    )
    local_sum = weight_sum
    local_weighted = weighted
    weight_sum, weighted = lax.psum((local_sum, local_weighted), "seq")
    attn = (weighted / weight_sum[..., None]).astype(jnp.bfloat16).reshape(flat_rows, head_cols)
    mid_rows = residual + head_total(jnp.dot(attn, w_out, preferred_element_type=jnp.float32))
    mlp_in = (mid_rows * mlp_scale).astype(jnp.bfloat16)
    mid_squares = jnp.sum(mid_rows * mid_rows, axis=-1)
    gate_up = jnp.dot(mlp_in, w_pair, preferred_element_type=jnp.float32)
    pair_sum, mid_sum = seq_total(gate_up, mid_squares)
    inv_mid = lax.rsqrt(mid_sum / D + EPSILON)[:, None]
    activated = (
        jax.nn.silu(pair_sum[:, :unit_cols] * inv_mid) * (pair_sum[:, unit_cols:] * inv_mid)
    ).astype(jnp.bfloat16)
    result = (
        mid_rows + head_total(jnp.dot(activated, w_down, preferred_element_type=jnp.float32))
    ).astype(jnp.bfloat16)
    hidden_out = result.reshape(step_count, requests, local_width)
    return (hidden_out, jnp.stack([key_new, value_new]))


MESH_ID = pl.DeviceIdType.MESH
LANES = 128
HALF_LANES = 64


def greet(axes):
    barrier = pltpu.get_barrier_semaphore()
    total = 0
    for axis, size in axes:
        me = lax.axis_index(axis)
        for step in range(1, size):
            pl.semaphore_signal(
                barrier,
                inc=1,
                device_id={axis: lax.rem(me + step, size)},
                device_id_type=MESH_ID,
            )
            total += 1
    return lambda: pl.semaphore_wait(barrier, total)


def send(source, target, axis, peer, send_sem, recv_sem):
    copy = pltpu.make_async_remote_copy(
        src_ref=source,
        dst_ref=target,
        send_sem=send_sem,
        recv_sem=recv_sem,
        device_id={axis: peer},
        device_id_type=MESH_ID,
    )
    copy.start()
    return copy


def place_of(n):
    me = lax.axis_index("seq")
    near = lax.rem(me, 2)
    far = me // 2
    half = n // 2

    def device(step, other):
        side = 1 - near if other else near
        return 2 * lax.rem(far + step + half, half) + side

    return me, half, device


def pair_scatter(n, make, put, get, near_out, near_in, far_out, far_in, sems):
    me, half, device = place_of(n)
    partner = device(0, True)
    near_send, near_recv, far_send, far_recv = sems
    order = list(range(1, half)) + [0]
    near = {}
    for d in order:
        put(near_out, d, make(device(d, True)))
        near[d] = send(
            near_out.at[d], near_in.at[d], "seq", partner, near_send.at[d], near_recv.at[d]
        )
    far = {}
    for d in range(1, half):
        peer = device(d, False)
        value = make(peer)
        near[d].wait_recv()
        put(far_out, d - 1, value + get(near_in, d))
        far[d] = send(
            far_out.at[d - 1], far_in.at[d - 1], "seq", peer, far_send.at[d - 1], far_recv.at[d - 1]
        )
    total = make(me)
    near[0].wait_recv()
    total = total + get(near_in, 0)
    for d in range(1, half):
        far[d].wait_recv()
        total = total + get(far_in, d - 1)
    return total, list(near.values()) + list(far.values())


def pair_gather(n, buffer, sems, arrive):
    me, half, device = place_of(n)
    partner = device(0, True)
    near_send, near_recv, far_send, far_recv = sems

    def share(index, peer, send_sem, recv_sem):
        return send(buffer.at[index], buffer.at[index], "seq", peer, send_sem, recv_sem)

    far = {}
    near = {}
    for d in range(1, half):
        far[d] = share(me, device(d, False), far_send.at[d - 1], far_recv.at[d - 1])
    near[0] = share(me, partner, near_send.at[0], near_recv.at[0])
    arrive(me)
    for d in range(1, half):
        far[d].wait_recv()
        index = device(-d, False)
        near[d] = share(index, partner, near_send.at[d], near_recv.at[d])
        arrive(index)
    for d in range(half):
        near[d].wait_recv()
        arrive(device(-d, True))
    return list(near.values()) + list(far.values())


def packed_width(width):
    return width + -(-width // (2 * LANES)) * LANES


def put_rows(ref, slot, value):
    width = value.shape[1]
    first = packed_width(width) - width
    ref[slot, :, :width] = value[:8]
    ref[slot, 0:4, width:] = value[8:12, :first]
    ref[slot, 4:8, width : 2 * width - first] = value[8:12, first:]
    if 2 * first > width:
        ref[slot, 4:8, 2 * width - first :] = jnp.zeros((4, 2 * first - width), value.dtype)


def get_rows(ref, slot, width):
    first = packed_width(width) - width
    value = ref[slot]
    rest = jnp.concatenate(
        [value[0:4, width:], value[4:8, width : 2 * width - first]], axis=1
    )
    return jnp.concatenate([value[:, :width], rest], axis=0)


def project_kernel(
    n,
    x_ref,
    gain_ref,
    wq_ref,
    wk_ref,
    wv_ref,
    cos_ref,
    sin_ref,
    out_ref,
    new_ref,
    partial,
    near_out,
    near_in,
    far_out,
    far_in,
    shared,
    *sems,
):
    me = lax.axis_index("seq")
    cols = wq_ref.shape[1]
    width = 3 * cols
    steps = out_ref.shape[1]
    rows = cos_ref.shape[1]
    all_here = greet((("seq", n),))
    x = x_ref[...].astype(jnp.float32)
    normed = (x * gain_ref[...].astype(jnp.float32)).astype(jnp.bfloat16)
    squares = jnp.sum(x * x, axis=-1, keepdims=True)

    def store(value, first, last):
        for j in range(n):
            partial[j, :, first:last] = value[j * rows : (j + 1) * rows]

    for index, weight in enumerate((wq_ref, wk_ref, wv_ref)):
        store(
            jnp.dot(normed, weight[...], preferred_element_type=jnp.float32),
            index * cols,
            (index + 1) * cols,
        )
    store(jnp.broadcast_to(squares, (x.shape[0], LANES)), width, width + LANES)
    all_here()
    total, copies = pair_scatter(
        n,
        lambda index: partial[index],
        put_rows,
        lambda ref, slot: get_rows(ref, slot, width + LANES),
        near_out,
        near_in,
        far_out,
        far_in,
        sems[:4],
    )
    inv_rms = lax.rsqrt(total[:, width : width + 1] / D + EPSILON)
    projected = total[:, :width] * inv_rms
    lane = lax.broadcasted_iota(jnp.int32, (rows, cols), 1)
    early = lax.rem(lane, HEAD_DIM) < HEAD_DIM // 2
    cosine = jnp.concatenate([cos_ref[me]] * (cols // HEAD_DIM), axis=1)
    sine = jnp.concatenate([sin_ref[me]] * (cols // HEAD_DIM), axis=1)

    def turn(vector):
        ahead = pltpu.roll(vector, cols - HEAD_DIM // 2, 1)
        behind = pltpu.roll(vector, HEAD_DIM // 2, 1)
        return vector * cosine + jnp.where(early, -ahead, behind) * sine

    spare = shared.shape[1] - rows

    def fill(value):
        return jnp.concatenate(
            [value, jnp.zeros((spare, value.shape[1]), jnp.float32)], axis=0
        ).astype(jnp.bfloat16)

    shared[me] = fill(turn(projected[:, :cols]))
    new_ref[:, :cols] = fill(turn(projected[:, cols : 2 * cols]))
    new_ref[:, cols:] = fill(projected[:, 2 * cols :])

    def arrive(index):
        held = shared[index].astype(jnp.float32)
        for i in range(rows // steps):
            out_ref[index * (rows // steps) + i] = held[i * steps : (i + 1) * steps]

    copies += pair_gather(n, shared, sems[4:], arrive)
    for copy in copies:
        copy.wait_send()


def head_masks(heads, cols):
    head_row = lax.broadcasted_iota(jnp.int32, (heads, cols), 0) * HEAD_DIM
    head_lane = lax.broadcasted_iota(jnp.int32, (heads, cols), 1)
    own = jnp.where((head_lane >= head_row) & (head_lane < head_row + HEAD_DIM), 1.0, 0.0)
    stat_lane = lax.broadcasted_iota(jnp.int32, (heads, LANES), 1)
    stat_row = lax.broadcasted_iota(jnp.int32, (heads, LANES), 0)
    pick_peak = jnp.where(stat_lane == stat_row, 1.0, 0.0)
    pick_sum = jnp.where(stat_lane == stat_row + HALF_LANES, 1.0, 0.0)
    return own, pick_peak, pick_sum


def attend_new(queries, keys, values, steps, heads):
    cols = queries[0].shape[1]
    own, pick_peak, pick_sum = head_masks(heads, cols)
    wide = jnp.concatenate(
        [value[t : t + 1] * own for value in queries for t in range(steps)], axis=0
    ).astype(jnp.bfloat16)
    scores = lax.dot_general(
        wide, keys, (((1,), (1,)), ((), ())), preferred_element_type=jnp.float32
    ) * (1.0 / math.sqrt(HEAD_DIM))
    query_row = lax.broadcasted_iota(jnp.int32, scores.shape, 0) // heads
    key_row = lax.broadcasted_iota(jnp.int32, scores.shape, 1)
    live = (key_row <= query_row) & (key_row // steps == query_row // steps)
    scores = jnp.where(live, scores, NEGATIVE)
    peak = jnp.max(scores, axis=-1, keepdims=True)
    weights = jnp.where(live, jnp.exp(scores - peak), 0.0)
    weight_sum = jnp.sum(weights, axis=-1, keepdims=True)
    coarse = weights.astype(jnp.bfloat16)
    fine = (weights - coarse.astype(jnp.float32)).astype(jnp.bfloat16)
    weighted = jnp.dot(coarse, values, preferred_element_type=jnp.float32) + jnp.dot(
        fine, values, preferred_element_type=jnp.float32
    )
    out = []
    for index in range(len(queries) * steps):
        part = slice(index * heads, (index + 1) * heads)
        out.append(
            jnp.concatenate(
                [
                    jnp.sum(weighted[part] * own, axis=0, keepdims=True),
                    jnp.sum(
                        peak[part] * pick_peak + weight_sum[part] * pick_sum,
                        axis=0,
                        keepdims=True,
                    ),
                ],
                axis=1,
            )
        )
    return jnp.concatenate(out, axis=0)


def attend_kernel(
    lengths_ref, pages_ref, query_ref, kv_ref, out_ref, pages, page_sem
):
    seq_index = lax.axis_index("seq")
    requests, steps = query_ref.shape[0], query_ref.shape[1]
    cols = pages.shape[-1]
    block_len = pages.shape[2]
    local_pages = page_sem.shape[1]
    page_rows = block_len // local_pages
    heads = cols // HEAD_DIM
    base = seq_index * block_len
    scale = 1.0 / math.sqrt(HEAD_DIM)

    def page_copy(b, p):
        return pltpu.make_async_copy(
            kv_ref.at[:, pages_ref[b, p]],
            pages.at[b, :, pl.ds(p * page_rows, page_rows)],
            page_sem.at[b, p],
        )

    def is_used(b):
        length = lengths_ref[b]
        return (base < length) & ((base < SINKS) | (base + block_len > length - WINDOW))

    @pl.loop(0, requests)
    def _(b):
        @pl.when(is_used(b))
        def _():
            for p in range(local_pages):
                page_copy(b, p).start()

    own, pick_peak, pick_sum = head_masks(heads, cols)
    row_step = lax.broadcasted_iota(jnp.int32, (steps * heads, block_len), 0) // heads
    place = base + lax.broadcasted_iota(jnp.int32, (steps * heads, block_len), 1)
    idle_lane = lax.broadcasted_iota(jnp.int32, (steps, cols + LANES), 1)
    idle = jnp.where((idle_lane >= cols) & (idle_lane < cols + HALF_LANES), NEGATIVE, 0.0)

    together = 4

    @pl.loop(0, requests // together)
    def _(block):
        for k in range(together):
            b = block * together + k

            @pl.when(is_used(b))
            def _():
                for p in range(local_pages):
                    page_copy(b, p).wait()

        batch = [block * together + k for k in range(together)]
        all_scores = []
        for b in batch:
            wide = jnp.concatenate(
                [query_ref[b, t : t + 1, :] * own for t in range(steps)], axis=0
            ).astype(jnp.bfloat16)
            all_scores.append(
                lax.dot_general(
                    wide,
                    pages[b, 0],
                    (((1,), (1,)), ((), ())),
                    preferred_element_type=jnp.float32,
                )
                * scale
            )
        parts = []
        for b, scores in zip(batch, all_scores):
            length = lengths_ref[b]
            live = (place < length) & ((place < SINKS) | (place > length + row_step - WINDOW))
            scores = jnp.where(live, scores, NEGATIVE)
            peak = jnp.max(scores, axis=-1, keepdims=True)
            weights = jnp.where(live, jnp.exp(scores - peak), 0.0)
            weight_sum = jnp.sum(weights, axis=-1, keepdims=True)
            coarse = weights.astype(jnp.bfloat16)
            fine = (weights - coarse.astype(jnp.float32)).astype(jnp.bfloat16)
            parts.append((peak, weight_sum, jnp.concatenate([coarse, fine], axis=0)))
        for b, (peak, weight_sum, pieces) in zip(batch, parts):
            both = jnp.dot(pieces, pages[b, 1], preferred_element_type=jnp.float32)
            weighted = both[: steps * heads] + both[steps * heads :]
            used = is_used(b)
            for t in range(steps):
                part = slice(t * heads, (t + 1) * heads)
                row = jnp.sum(weighted[part] * own, axis=0, keepdims=True)
                stat = jnp.sum(
                    peak[part] * pick_peak + weight_sum[part] * pick_sum, axis=0, keepdims=True
                )
                out_ref[b, t : t + 1, :] = jnp.where(
                    used, jnp.concatenate([row, stat], axis=1), idle[t : t + 1]
                )


def finish_kernel(
    n,
    m,
    att_ref,
    x_ref,
    gain_ref,
    wo_ref,
    wg_ref,
    wu_ref,
    wd_ref,
    query_ref,
    fresh_ref,
    out_ref,
    cache_ref,
    fresh_all,
    chunks,
    landed,
    shared,
    flat,
    mid_landed,
    mid_all,
    near_out,
    near_in,
    far_out,
    far_in,
    square_out,
    square_landed,
    acts,
    down_landed,
    last,
    send_a,
    recv_a,
    send_s,
    recv_s,
    *sems,
):
    me = lax.axis_index("seq")
    rank = lax.axis_index("tp")
    tp_sems, seq_sems = sems[:8], sems[8:]
    steps = att_ref.shape[1]
    cols = wo_ref.shape[0]
    group = mid_all.shape[1]
    flat_rows = flat.shape[0]
    local_width = flat.shape[1]
    units = acts.shape[2]
    rows = flat_rows // n
    per = rows // steps
    all_here = greet((("seq", n), ("tp", m)))
    for j in range(n):
        put_rows(chunks, j, jnp.concatenate([att_ref[j * per + i] for i in range(per)], axis=0))
    all_here()
    copies = []
    for d in range(1, n):
        peer = lax.rem(me + d, n)
        copies.append(
            send(chunks.at[peer], landed.at[d - 1], "seq", peer, send_a.at[d - 1], recv_a.at[d - 1])
        )
    heads = cols // HEAD_DIM
    fresh = attend_new(
        [query_ref[me * per + i] for i in range(per)],
        fresh_ref[:, :cols],
        fresh_ref[:, cols:],
        steps,
        heads,
    )
    fresh_all[me] = fresh_ref[...]
    for copy in copies:
        copy.wait_recv()
    arrived = [fresh, get_rows(chunks, me, cols + LANES)] + [
        get_rows(landed, d - 1, cols + LANES) for d in range(1, n)
    ]
    stats = [value[:, cols:] for value in arrived]
    lane = lax.broadcasted_iota(jnp.int32, (rows, LANES), 1)
    is_peak = lane < HALF_LANES
    peaks = [jnp.where(is_peak, value, 0.0) for value in stats]
    top = functools.reduce(jnp.maximum, peaks)
    factors = [jnp.exp(value - top) for value in peaks]
    sums = [pltpu.roll(value, HALF_LANES, 1) for value in stats]
    total_sum = functools.reduce(lambda a, b: a + b, [f * s for f, s in zip(factors, sums)])
    inverse = 1.0 / jnp.where(lane < heads, total_sum, 1.0)
    spread_row = lax.broadcasted_iota(jnp.int32, (LANES, cols), 0) * HEAD_DIM
    spread_lane = lax.broadcasted_iota(jnp.int32, (LANES, cols), 1)
    spread = jnp.where(
        (spread_lane >= spread_row) & (spread_lane < spread_row + HEAD_DIM), 1.0, 0.0
    ).astype(jnp.bfloat16)
    attn = jnp.zeros((rows, cols), jnp.float32)
    blank = jnp.zeros((16 - rows, LANES), jnp.float32)
    rest = jnp.concatenate(
        [
            jnp.concatenate([jnp.where(lane < heads, factor * inverse, 0.0), blank], axis=0)
            for factor in factors
        ],
        axis=0,
    )
    shares = 0.0
    for _ in range(3):
        piece = rest.astype(jnp.bfloat16)
        rest = rest - piece.astype(jnp.float32)
        shares = shares + jnp.dot(piece, spread, preferred_element_type=jnp.float32)
    for index, value in enumerate(arrived):
        attn = attn + value[:, :cols] * shares[index * 16 : index * 16 + rows]
    padded = shared.shape[1]
    shared[me] = jnp.concatenate(
        [attn, jnp.zeros((padded - rows, cols), jnp.float32)], axis=0
    ).astype(jnp.bfloat16)
    copies += pair_gather(n, shared, seq_sems[:4], lambda index: None)
    _, half, device = place_of(n)
    partner = device(0, True)
    near_send, near_recv, far_send, far_recv = seq_sems[12:16]

    def pass_on(index, peer, send_sem, recv_sem):
        return send(fresh_all.at[index], fresh_all.at[index], "seq", peer, send_sem, recv_sem)

    cache_far = {}
    for d in range(1, half):
        cache_far[d] = pass_on(me, device(d, False), far_send.at[d - 1], far_recv.at[d - 1])
    product = jnp.dot(
        shared[...].reshape(n * padded, cols), wo_ref[...], preferred_element_type=jnp.float32
    )
    for j in range(n):
        flat[j * rows : (j + 1) * rows, :] = product[j * padded : j * padded + rows]

    def tp_scatter(target, send_sem, recv_sem):
        started = []
        for d in range(1, m):
            peer = lax.rem(rank + d, m)
            first = pl.multiple_of(peer * group, group)
            started.append(
                send(
                    flat.at[pl.ds(first, group)],
                    target.at[d - 1],
                    "tp",
                    peer,
                    send_sem.at[d - 1],
                    recv_sem.at[d - 1],
                )
            )
        total = flat[pl.ds(pl.multiple_of(rank * group, group), group), :]
        for d in range(1, m):
            started[d - 1].wait_recv()
            total = total + target[d - 1]
        for copy in started:
            copy.wait_send()
        return total

    def tp_gather(buffer, send_sem, recv_sem):
        started = []
        for d in range(1, m):
            peer = lax.rem(rank + d, m)
            started.append(
                send(
                    buffer.at[rank],
                    buffer.at[rank],
                    "tp",
                    peer,
                    send_sem.at[d - 1],
                    recv_sem.at[d - 1],
                )
            )
        for copy in started:
            copy.wait()

    own_rows = pl.ds(pl.multiple_of(rank * group, group), group)
    mid_own = x_ref[own_rows, :] + tp_scatter(mid_landed, *tp_sems[0:2])
    mid_all[rank] = mid_own
    tp_gather(mid_all, *tp_sems[2:4])
    mid = mid_all[...].reshape(flat_rows, local_width)
    mlp_in = (mid * gain_ref[...].astype(jnp.float32)).astype(jnp.bfloat16)
    square_out[...] = lax.dot_general(
        jnp.ones((8, local_width), jnp.float32),
        mid * mid,
        (((1,), (1,)), ((), ())),
        precision=lax.Precision.HIGHEST,
        preferred_element_type=jnp.float32,
    )
    squares = []
    for d in range(1, n):
        peer = lax.rem(me + d, n)
        squares.append(
            send(square_out, square_landed.at[d - 1], "seq", peer, send_s.at[d - 1], recv_s.at[d - 1])
        )

    def pair(index):
        span = pl.ds(pl.multiple_of(index * units, units), units)
        return jnp.concatenate(
            [
                jnp.dot(mlp_in, wg_ref[:, span], preferred_element_type=jnp.float32),
                jnp.dot(mlp_in, wu_ref[:, span], preferred_element_type=jnp.float32),
            ],
            axis=1,
        )

    def put(ref, slot, value):
        ref[slot] = value.astype(ref.dtype)

    pair_total, pairs = pair_scatter(
        n,
        pair,
        put,
        lambda ref, slot: ref[slot].astype(jnp.float32),
        near_out,
        near_in,
        far_out,
        far_in,
        seq_sems[4:8],
    )
    copies += pairs
    for copy in squares:
        copy.wait()
    square_sum = square_out[...]
    for d in range(1, n):
        square_sum = square_sum + square_landed[d - 1]
    column = lax.dot_general(
        square_sum,
        jnp.full((8, units), 0.125, jnp.float32),
        (((0,), (0,)), ((), ())),
        precision=lax.Precision.HIGHEST,
        preferred_element_type=jnp.float32,
    )
    inv_mid = lax.rsqrt(column / D + EPSILON)
    gate = pair_total[:, :units] * inv_mid
    act = gate / (1.0 + jnp.exp(-gate)) * (pair_total[:, units:] * inv_mid)
    acts[me] = act.astype(jnp.bfloat16)
    flat[...] = jnp.zeros_like(flat)

    def down(index):
        span = pl.ds(pl.multiple_of(index * units, units), units)
        flat[...] += jnp.dot(acts[index], wd_ref[span, :], preferred_element_type=jnp.float32)

    copies += pair_gather(n, acts, seq_sems[8:12], down)
    for copy in copies:
        copy.wait_send()
    cache_near = [pass_on(me, partner, near_send.at[0], near_recv.at[0])]
    for d in range(1, half):
        cache_far[d].wait_recv()
        cache_near.append(
            pass_on(device(-d, False), partner, near_send.at[d], near_recv.at[d])
        )
    last[rank] = (mid_own + tp_scatter(down_landed, *tp_sems[4:6])).astype(jnp.bfloat16)
    tp_gather(last, *tp_sems[6:8])
    out_ref[...] = last[...]
    for copy in cache_near:
        copy.wait()
    for copy in cache_far.values():
        copy.wait_send()
    cache_ref[...] = fresh_all[...]


def fused_body(
    n,
    m,
    hidden_in,
    attn_gain,
    w_query,
    w_key,
    w_value,
    w_out,
    mlp_gain,
    w_gate,
    w_up,
    w_down,
    kv_pages,
    lengths,
    group_ids,
    shared_table,
    own_table,
):
    seq_index = lax.axis_index("seq")
    steps, requests, local_width = hidden_in.shape
    cols = w_query.shape[1]
    flat_rows = steps * requests
    rows = flat_rows // n
    padded = -(-rows // 16) * 16
    group = flat_rows // m
    units = w_gate.shape[1] // n
    page_rows = kv_pages.shape[2]
    local_pages = own_table.shape[1]
    block_len = local_pages * page_rows
    group_count, prompt_pages = shared_table.shape
    f32, bf16 = jnp.float32, jnp.bfloat16

    logical = seq_index * local_pages + jnp.arange(local_pages, dtype=jnp.int32)
    group_pick = (group_ids[:, None] == jnp.arange(group_count, dtype=jnp.int32)[None, :]).astype(
        jnp.int32
    )
    group_rows = jnp.sum(group_pick[:, :, None] * shared_table[None, :, :], axis=1)
    column_pick = (logical[:, None] == jnp.arange(prompt_pages, dtype=jnp.int32)[None, :]).astype(
        jnp.int32
    )
    shared_local = jnp.sum(group_rows[:, None, :] * column_pick[None, :, :], axis=2)
    physical = jnp.where(logical[None, :] < prompt_pages, shared_local, own_table)

    x = jnp.transpose(hidden_in, (1, 0, 2)).reshape(flat_rows, local_width)
    halfway = HEAD_DIM // 2
    frequency = ROPE_BASE ** (-(jnp.arange(halfway, dtype=f32) * 2.0 / HEAD_DIM))
    where_now = (lengths[:, None] + jnp.arange(steps, dtype=jnp.int32)[None, :]).reshape(-1)
    angles = where_now[:, None].astype(f32) * frequency
    cosine = jnp.tile(jnp.cos(angles), (1, 2)).reshape(n, rows, HEAD_DIM)
    sine = jnp.tile(jnp.sin(angles), (1, 2)).reshape(n, rows, HEAD_DIM)

    vmem = pl.BlockSpec(memory_space=pltpu.VMEM)
    smem = pl.BlockSpec(memory_space=pltpu.SMEM)
    dma = pltpu.SemaphoreType.DMA
    wide = 3 * cols
    half = n // 2
    pair_sems = [dma((half,))] * 2 + [dma((half - 1,))] * 2
    queries, fresh = pl.pallas_call(
        functools.partial(project_kernel, n),
        out_shape=(
            jax.ShapeDtypeStruct((requests, steps, cols), f32),
            jax.ShapeDtypeStruct((padded, 2 * cols), bf16),
        ),
        in_specs=[vmem] * 7,
        out_specs=(vmem, vmem),
        scratch_shapes=[
            pltpu.VMEM((n, rows, wide + LANES), f32),
            pltpu.VMEM((half, 8, packed_width(wide + LANES)), f32),
            pltpu.VMEM((half, 8, packed_width(wide + LANES)), f32),
            pltpu.VMEM((half - 1, 8, packed_width(wide + LANES)), f32),
            pltpu.VMEM((half - 1, 8, packed_width(wide + LANES)), f32),
            pltpu.VMEM((n, padded, cols), bf16),
        ]
        + pair_sems * 2,
        compiler_params=pltpu.CompilerParams(
            collective_id=0, has_side_effects=True, vmem_limit_bytes=48 << 20
        ),
    )(x, attn_gain.reshape(1, -1), w_query, w_key, w_value, cosine, sine)
    attended = pl.pallas_call(
        attend_kernel,
        out_shape=jax.ShapeDtypeStruct((requests, steps, cols + LANES), f32),
        in_specs=[smem, smem, vmem, pl.BlockSpec(memory_space=pl.ANY)],
        out_specs=vmem,
        scratch_shapes=[
            pltpu.VMEM((requests, 2, block_len, cols), bf16),
            dma((requests, local_pages)),
        ],
        compiler_params=pltpu.CompilerParams(vmem_limit_bytes=48 << 20),
    )(lengths, physical, queries, kv_pages)

    result, caches = pl.pallas_call(
        functools.partial(finish_kernel, n, m),
        out_shape=(
            jax.ShapeDtypeStruct((m, group, local_width), bf16),
            jax.ShapeDtypeStruct((n, padded, 2 * cols), bf16),
        ),
        in_specs=[vmem] * 9,
        out_specs=(vmem, vmem),
        scratch_shapes=[
            pltpu.VMEM((n, padded, 2 * cols), bf16),
            pltpu.VMEM((n, 8, packed_width(cols + LANES)), f32),
            pltpu.VMEM((n - 1, 8, packed_width(cols + LANES)), f32),
            pltpu.VMEM((n, padded, cols), bf16),
            pltpu.VMEM((flat_rows, local_width), f32),
            pltpu.VMEM((m - 1, group, local_width), f32),
            pltpu.VMEM((m, group, local_width), f32),
            pltpu.VMEM((half, flat_rows, 2 * units), bf16),
            pltpu.VMEM((half, flat_rows, 2 * units), bf16),
            pltpu.VMEM((half - 1, flat_rows, 2 * units), bf16),
            pltpu.VMEM((half - 1, flat_rows, 2 * units), bf16),
            pltpu.VMEM((8, flat_rows), f32),
            pltpu.VMEM((n - 1, 8, flat_rows), f32),
            pltpu.VMEM((n, flat_rows, units), bf16),
            pltpu.VMEM((m - 1, group, local_width), f32),
            pltpu.VMEM((m, group, local_width), bf16),
        ]
        + [dma((n - 1,))] * 4
        + [dma((m - 1,))] * 8
        + pair_sems * 4,
        compiler_params=pltpu.CompilerParams(
            collective_id=1, has_side_effects=True, vmem_limit_bytes=48 << 20
        ),
    )(
        attended,
        x.astype(f32),
        mlp_gain.reshape(1, -1),
        w_out,
        w_gate,
        w_up,
        w_down,
        queries,
        fresh,
    )
    new_cache = jnp.transpose(
        caches[:, :rows].reshape(requests, steps, 2, cols), (2, 1, 0, 3)
    )
    hidden_out = jnp.transpose(result.reshape(requests, steps, local_width), (1, 0, 2))
    return (hidden_out, new_cache)


def fits(n, m):
    flat_rows = 96
    return (
        n % 2 == 0
        and n > 2
        and m > 1
        and flat_rows == n * 12
        and flat_rows % (m * 8) == 0
        and D // m % LANES == 0
        and D // m // HEAD_DIM <= 8
    )


def solution(mesh):
    n, m = mesh.shape["seq"], mesh.shape["tp"]
    chosen = functools.partial(fused_body, n, m) if fits(n, m) else body
    return jax.shard_map(
        chosen,
        mesh=mesh,
        in_specs=(
            P(None, None, "seq"),
            P("seq"),
            P("seq", "tp"),
            P("seq", "tp"),
            P("seq", "tp"),
            P("tp", "seq"),
            P("seq"),
            P("seq", "tp"),
            P("seq", "tp"),
            P("tp", "seq"),
            P(None, "seq", None, "tp"),
            P(),
            P(),
            P(),
            P(None, "seq"),
        ),
        out_specs=(P(None, None, "seq"), P(None, None, None, "tp")),
        check_vma=False,
    )
```
